256 devices in a mesh: grp: 2 (over core), tok: 32 (over z, y), head: 4 (over x).
Axes of the slice: x: 4, y: 4, z: 8, core: 2. Of those that a mesh axis runs over, the one named last changes fastest.
Arguments:
- hidden_in: bfloat16 [2, 4096, 2560], P('grp', 'tok', 'head'), may hold values from -6 to 6
- attn_gain: bfloat16 [2560], replicated, may hold values from 0.5 to 1.5
- w_query: bfloat16 [2560, 2560], P('grp', 'head'), may hold values from -0.125 to 0.125
- key_projection_weight: bfloat16 [2560, 512], P('grp', 'head'), may hold values from -0.25 to 0.25
- value_projection_weight: bfloat16 [2560, 512], P('grp', 'head'), may hold values from -0.125 to 0.125
- w_out: bfloat16 [2560, 2560], P('grp', 'head'), may hold values from -0.125 to 0.125
- prefix_keys: bfloat16 [2, 2048, 4, 128], P('grp', 'tok', 'head'), may hold values from -91 to 91
- cached_prefix_values: bfloat16 [2, 2048, 4, 128], P('grp', 'tok', 'head'), may hold values from -6 to 6
- request_lengths: int32 [2, 16], P('grp'), may hold values from 1 to 1024, 4096 in all within a row
- moe_gain: bfloat16 [2560], replicated, may hold values from 0.5 to 1.5
- expert_ids: int32 [2, 4096, 6], P('grp', 'tok'), may hold values from 0 to 63, all different within a row; in each aligned block of 128 rows (0 to 127, 128 to 255, ..., all dimensions but the last counted through in order) at most 16 rows name the same one
- route_weights: float32 [2, 4096, 6], P('grp', 'tok'), may hold values from 0.05 to 0.3
- w_gate: bfloat16 [64, 2560, 1536], P(('grp', 'tok'), None, 'head'), may hold values from -0.125 to 0.125
- w_up: bfloat16 [64, 2560, 1536], P(('grp', 'tok'), None, 'head'), may hold values from -0.125 to 0.125
- w_down: bfloat16 [64, 1536, 2560], P(('grp', 'tok'), None, 'head'), may hold values from -0.15625 to 0.15625
Outputs:
- hidden_out: bfloat16 [2, 4096, 2560], P('grp', 'tok', 'head')
The draws below stay inside these ranges and needn't reach their ends.
Inputs may be any that keep to these rules, and one draw needn't show every extreme that they name: `expert_ids`: each token names 6 different experts. Among the tokens of one device (aligned blocks of 128 tokens of a group) no expert is named more than 16 times.
All inputs are finite; a program needn't handle non-finite values.
Results may differ from the reference program's by a relative error of at most 0.011.
Values may be sent and summed in bfloat16 or wider, within the bound.
A program may use at most 64 MiB of HBM per device.

```python
import math
import jax
import jax.numpy as jnp
import numpy as np
from jax import lax

MODEL_DIMENSION = 2560
QUERY_HEADS = 20
KEY_VALUE_HEADS = 4
HEAD_SIZE = 128
FE = 1536
TOP = 6
TOK_DEV = 128
REQS = 16
REQUEST_GROUPS = 2
EXPERTS = 64
SUFFIX_LENGTH = 4096
PREFIX_LENGTH = 2048
L_MAX = 1024
CAP = 16
N_TOK = 32


def draw_prefix_keys(key, part):
    tensor_shape = (REQUEST_GROUPS, PREFIX_LENGTH, KEY_VALUE_HEADS, HEAD_SIZE)
    drawn = 2.0 * jax.random.truncated_normal(key, -6.0, 6.0, tensor_shape, jnp.float32)
    return drawn.astype(jnp.bfloat16)


def shard_levels(key, extent, shards, low, largest):
    gain = 1.0
    for axis_at, blocks in shards:
        draws = jax.random.uniform(jax.random.fold_in(jax.random.fold_in(key, 6), axis_at), (blocks,), jnp.float32, low / len(shards), largest / len(shards))
        gain = gain * jnp.repeat(jnp.exp(draws), extent[axis_at] // blocks).reshape((-1,) + (1,) * (len(extent) - 1 - axis_at))
    return gain


def split_up(number_of, total, limit, slope):
    loads = [(1 << 20) // math.isqrt(standing ** slope) + 1 for standing in range(2, number_of + 1)]
    rest, given = total - limit - (number_of - 1), [1] * (number_of - 1)
    while rest > 0:
        movable = [i for i in range(number_of - 1) if given[i] < limit]
        mass, remaining = sum([loads[i] for i in movable]), rest
        for i in movable:
            extra = min(limit - given[i], max(1, remaining * loads[i] // mass), rest)
            given[i] = given[i] + extra
            rest = rest - extra
    return np.array([limit] + given)


def ragged(stream_key, number_of, total, bound, skew):
    if number_of == 2:
        one = jax.random.randint(stream_key, (), max(1, total - bound), min(bound, total - 1) + 1)
        return jnp.stack([one, total - one])
    tallies = jnp.asarray(split_up(number_of, total, bound, skew), jnp.int32)
    couples = (number_of - 1) // 2
    donor, receiver = tallies[1:1 + 2 * couples:2], tallies[2:2 + 2 * couples:2]
    slack = jnp.minimum(donor - 1, bound - receiver)
    passed = jax.random.randint(jax.random.fold_in(stream_key, 1), (couples,), 0, 1 << 20) % (slack + 1)
    tallies = tallies.at[1:1 + 2 * couples:2].set(donor - passed).at[2:2 + 2 * couples:2].set(receiver + passed)
    return tallies[jax.random.permutation(jax.random.fold_in(stream_key, 2), number_of)]


def assign_block(own_key, own, number, rows, number_of, top, limit, slope):
    ranking = jax.random.permutation(own_key, number_of)
    crowded, common = portions_of(number_of, rows * top, limit, slope, True), portions_of(number_of, rows * top, limit, slope, False)
    places = jnp.arange(number_of)

    def named(sizes, rotation):
        used = int((sizes > 0).sum())
        fixed = max(1, used // 4)
        moved = fixed + (places - fixed + rotation * (used - fixed)) % max(1, number_of - fixed)
        return jnp.zeros((number_of,), jnp.int32).at[ranking[jnp.where(places < fixed, places, moved)]].set(jnp.asarray(sizes, jnp.int32))

    sizes = jnp.where(number % 4 == 0, named(crowded, number // 4), named(common, number - number // 4 - 1))
    mixed = jax.random.permutation(jax.random.fold_in(own, 3), number_of)
    giver, receiver = mixed[0:number_of // 2 * 2:2], mixed[1:number_of // 2 * 2:2]
    room = jnp.minimum(sizes[giver] - 1, limit - sizes[receiver]) // 2
    room = jnp.where((giver == ranking[0]) | (receiver == ranking[0]) | (sizes[receiver] == 0), 0, jnp.maximum(room, 0))
    moved = jax.random.randint(jax.random.fold_in(own, 4), (number_of // 2,), 0, 1 << 20) % (room + 1)
    sizes = sizes.at[giver].add(-moved).at[receiver].add(moved)
    members = jnp.searchsorted(jnp.cumsum(sizes), jnp.arange(rows * top), side="right").astype(jnp.int32)
    grid = members.reshape(top, rows).T
    grid = grid[jax.random.permutation(jax.random.fold_in(own, 1), rows)]
    rotation = jax.random.randint(jax.random.fold_in(own, 2), (rows, 1), 0, top)
    return jnp.take_along_axis(grid, (jnp.arange(top)[None, :] + rotation) % top, axis=1)


def portions_of(amount, total, reach, lean, full):
    portions = [(1 << 20) // math.isqrt(grade ** lean) + 1 for grade in range(1, amount + 1)]
    largest = reach if full else min(reach, max(-(-total // amount), total * portions[0] // sum(portions)))
    least = 1 if total - largest >= amount - 1 else 0
    counts, rest = [largest] + [least] * (amount - 1), total - largest - least * (amount - 1)
    while rest > 0:
        movable = [i for i in range(1, amount) if counts[i] < largest] or [i for i in range(1, amount) if counts[i] < reach]
        pool, left = sum([portions[i] for i in movable]), rest
        for i in movable:
            extra = min(reach - counts[i], max(1, left * portions[i] // pool), rest)
            counts[i] = counts[i] + extra
            rest = rest - extra
    return np.array(counts)


def centred(stream_key, extent, width, reach, shards=(), kind=jnp.bfloat16):
    values = width * jax.random.normal(stream_key, extent, jnp.float32)
    if shards:
        values = values * shard_levels(stream_key, extent, shards, -0.22, 0.18)
    return jnp.clip(values, -reach, reach).astype(kind)


def setup_inputs(seed: int = 0) -> dict:
    splits = jax.random.split(jax.random.key(seed), 16)
    hidden_in = centred(splits[0], (REQUEST_GROUPS, SUFFIX_LENGTH, MODEL_DIMENSION), 1.0, 6.0, ((0, 2), (1, 32), (2, 4)))
    attn_gain = jnp.clip(1.0 + 0.1 * jax.random.normal(splits[1], (MODEL_DIMENSION,), jnp.float32), 0.5, 1.5).astype(jnp.bfloat16)
    w_query = centred(splits[2], (MODEL_DIMENSION, QUERY_HEADS * HEAD_SIZE), MODEL_DIMENSION ** -0.5, 0.125, ((0, 2), (1, 4)))
    key_projection_weight = centred(splits[3], (MODEL_DIMENSION, KEY_VALUE_HEADS * HEAD_SIZE), (MODEL_DIMENSION // 4) ** -0.5, 0.25, ((0, 2), (1, 4)))
    value_projection_weight = centred(splits[4], (MODEL_DIMENSION, KEY_VALUE_HEADS * HEAD_SIZE), MODEL_DIMENSION ** -0.5, 0.125, ((0, 2), (1, 4)))
    w_out = centred(splits[5], (MODEL_DIMENSION, QUERY_HEADS * HEAD_SIZE), (QUERY_HEADS * HEAD_SIZE) ** -0.5, 0.125, ((0, 2), (1, 4)))
    prefix_keys = draw_prefix_keys(jax.random.fold_in(splits[15], 71), 0)
    cached_prefix_values = centred(splits[7], (REQUEST_GROUPS, PREFIX_LENGTH, KEY_VALUE_HEADS, HEAD_SIZE), 1.0, 6.0, ((0, 2), (1, 32), (2, 4)))
    request_lengths = jax.vmap(lambda own: ragged(own, REQS, SUFFIX_LENGTH, L_MAX, 2))(jax.random.split(splits[8], REQUEST_GROUPS)).reshape((REQUEST_GROUPS, REQS)).astype(jnp.int32)
    moe_gain = jnp.clip(1.0 + 0.1 * jax.random.normal(splits[9], (MODEL_DIMENSION,), jnp.float32), 0.5, 1.5).astype(jnp.bfloat16)
    expert_ids_keys = jax.random.split(jax.random.fold_in(splits[10], 1), REQUEST_GROUPS * SUFFIX_LENGTH // TOK_DEV)
    expert_ids_turns = jax.random.permutation(jax.random.fold_in(splits[10], 3), REQUEST_GROUPS * SUFFIX_LENGTH // TOK_DEV)
    expert_ids = jax.vmap(lambda own, number: assign_block(jax.random.fold_in(splits[10], 2), own, number, TOK_DEV, EXPERTS, TOP, CAP, 2))(expert_ids_keys, expert_ids_turns).reshape((REQUEST_GROUPS, SUFFIX_LENGTH, TOP))
    route_weights = jnp.clip(0.05 + 0.25 * jax.random.uniform(splits[11], (REQUEST_GROUPS, SUFFIX_LENGTH, TOP), jnp.float32) ** shard_levels(splits[11], (REQUEST_GROUPS, SUFFIX_LENGTH, TOP), ((0, 2), (1, 32)), -0.2, 0.2), 0.05, 0.3)
    w_gate = centred(splits[12], (EXPERTS, MODEL_DIMENSION, FE), MODEL_DIMENSION ** -0.5, 0.125, ((0, 64), (2, 4)))
    w_up = centred(splits[13], (EXPERTS, MODEL_DIMENSION, FE), MODEL_DIMENSION ** -0.5, 0.125, ((0, 64), (2, 4)))
    w_down = centred(splits[14], (EXPERTS, FE, MODEL_DIMENSION), FE ** -0.5, 0.15625, ((0, 64), (2, 4)))
    return {"hidden_in": hidden_in, "attn_gain": attn_gain, "w_query": w_query, "key_projection_weight": key_projection_weight, "value_projection_weight": value_projection_weight, "w_out": w_out, "prefix_keys": prefix_keys, "cached_prefix_values": cached_prefix_values, "request_lengths": request_lengths, "moe_gain": moe_gain, "expert_ids": expert_ids, "route_weights": route_weights, "w_gate": w_gate, "w_up": w_up, "w_down": w_down}


ROPE_BASE = 500000.0
NORM_EPS = 1e-06
MASKED = -1e+30

def rms_norm(values_in, gain_vector):
    widened = values_in.astype(jnp.float32)
    mean_sq = lax.optimization_barrier(jnp.mean(widened * widened, axis=-1, keepdims=True))
    return (widened * lax.rsqrt(mean_sq + NORM_EPS) * gain_vector.astype(jnp.float32)).astype(jnp.bfloat16)

def apply_rotary(product, token_positions):
    half_dim = product.shape[-1] // 2
    frequency = jnp.exp(jnp.arange(half_dim, dtype=jnp.float32) * (-2.0 * math.log(ROPE_BASE) / product.shape[-1]))
    angles = token_positions.astype(jnp.float32)[:, None] * frequency[None, :]
    cosine = jnp.cos(angles)[:, None, :]
    sine_part = jnp.sin(angles)[:, None, :]
    first_half = product[..., :half_dim]
    second_half = product[..., half_dim:]
    turned = jnp.concatenate([first_half * cosine - second_half * sine_part, second_half * cosine + first_half * sine_part], axis=-1)
    return turned.astype(jnp.bfloat16)

def reference(hidden_in, attn_gain, w_query, key_projection_weight, value_projection_weight, w_out, prefix_keys, cached_prefix_values, request_lengths, moe_gain, expert_ids, route_weights, w_gate, w_up, w_down):
    scale = HEAD_SIZE ** (-0.5)
    group_length = QUERY_HEADS // KEY_VALUE_HEADS
    mids = []
    for grp_index in range(REQUEST_GROUPS):
        stream = hidden_in[grp_index]
        attention_input = rms_norm(stream, attn_gain)
        lengths = request_lengths[grp_index]
        request_ends = jnp.cumsum(lengths).astype(jnp.int32)
        starts = (request_ends - lengths).astype(jnp.int32)
        token_index = jnp.arange(SUFFIX_LENGTH, dtype=jnp.int32)
        own_start = lax.optimization_barrier(jnp.max(jnp.where(starts[None, :] <= token_index[:, None], starts[None, :], 0), axis=1)).astype(jnp.int32)
        token_positions = (PREFIX_LENGTH + token_index - own_start).astype(jnp.int32)
        query = apply_rotary(jnp.dot(attention_input, w_query, preferred_element_type=jnp.float32).reshape(SUFFIX_LENGTH, QUERY_HEADS, HEAD_SIZE), token_positions)
        request_suffix_keys = apply_rotary(jnp.dot(attention_input, key_projection_weight, preferred_element_type=jnp.float32).reshape(SUFFIX_LENGTH, KEY_VALUE_HEADS, HEAD_SIZE), token_positions)
        request_suffix_values = jnp.dot(attention_input, value_projection_weight, preferred_element_type=jnp.float32).astype(jnp.bfloat16).reshape(SUFFIX_LENGTH, KEY_VALUE_HEADS, HEAD_SIZE)
        visible = (token_index[None, :] >= own_start[:, None]) & (token_index[None, :] <= token_index[:, None])
        cache_keys = prefix_keys[grp_index]
        cache_values = cached_prefix_values[grp_index]

        def one_head(head_number):
            kv_index = head_number // group_length
            head_query = lax.dynamic_index_in_dim(query, head_number, axis=1, keepdims=False)
            pre_keys = lax.dynamic_index_in_dim(cache_keys, kv_index, axis=1, keepdims=False)
            pre_values = lax.dynamic_index_in_dim(cache_values, kv_index, axis=1, keepdims=False)
            suf_keys = lax.dynamic_index_in_dim(request_suffix_keys, kv_index, axis=1, keepdims=False)
            suf_values = lax.dynamic_index_in_dim(request_suffix_values, kv_index, axis=1, keepdims=False)
            score_pre = jnp.dot(head_query, pre_keys.T, preferred_element_type=jnp.float32) * scale
            score_suf = jnp.where(visible, jnp.dot(head_query, suf_keys.T, preferred_element_type=jnp.float32) * scale, MASKED)
            row_max = jnp.maximum(lax.optimization_barrier(jnp.max(score_pre, axis=1)), lax.optimization_barrier(jnp.max(score_suf, axis=1)))[:, None]
            prob_pre = jnp.exp(score_pre - row_max)
            prob_suf = jnp.where(visible, jnp.exp(score_suf - row_max), 0.0)
            denominator = lax.optimization_barrier(jnp.sum(prob_pre, axis=1)) + lax.optimization_barrier(jnp.sum(prob_suf, axis=1))
            numerator = jnp.dot(prob_pre.astype(jnp.bfloat16), pre_values, preferred_element_type=jnp.float32)
            numerator = numerator + jnp.dot(prob_suf.astype(jnp.bfloat16), suf_values, preferred_element_type=jnp.float32)
            return (numerator / denominator[:, None]).astype(jnp.bfloat16)
        heads_out = lax.map(one_head, jnp.arange(QUERY_HEADS, dtype=jnp.int32))
        attended = jnp.transpose(heads_out, (1, 0, 2)).reshape(SUFFIX_LENGTH, QUERY_HEADS * HEAD_SIZE)
        projected = jnp.dot(attended, w_out.T, preferred_element_type=jnp.float32)
        mids.append((stream.astype(jnp.float32) + projected).astype(jnp.bfloat16))
    mid = jnp.stack(mids)
    moe_in = rms_norm(mid, moe_gain)
    blocks = REQUEST_GROUPS * N_TOK
    per_block = TOK_DEV * TOP
    chosen = expert_ids.reshape(blocks, per_block).astype(jnp.int32)
    onehot = (chosen[:, :, None] == jnp.arange(EXPERTS, dtype=jnp.int32)[None, None, :]).astype(jnp.int32)
    running_count = jnp.cumsum(onehot, axis=1).astype(jnp.int32)
    slot_rank = (lax.optimization_barrier(jnp.sum(onehot * running_count, axis=2)) - 1).astype(jnp.int32)
    block_index = jnp.broadcast_to(jnp.arange(blocks, dtype=jnp.int32)[:, None], (blocks, per_block))
    token_of = (block_index * TOK_DEV + jnp.arange(per_block, dtype=jnp.int32)[None, :] // TOP).astype(jnp.int32)
    table = jnp.full((EXPERTS, blocks, CAP), blocks * TOK_DEV, jnp.int32).at[chosen, block_index, slot_rank].set(token_of)
    flat_in = moe_in.reshape(blocks * TOK_DEV, MODEL_DIMENSION)

    def one_expert(operands):
        rows_index, gate_matrix, up_matrix, down_matrix = operands
        flat_rows = jnp.take(flat_in, rows_index.reshape(-1), axis=0, mode='fill', fill_value=0)
        gate_act = jnp.dot(flat_rows, gate_matrix, preferred_element_type=jnp.float32)
        up_act = jnp.dot(flat_rows, up_matrix, preferred_element_type=jnp.float32)
        hidden = (jax.nn.silu(gate_act) * up_act).astype(jnp.bfloat16)
        return jnp.dot(hidden, down_matrix, preferred_element_type=jnp.float32).astype(jnp.bfloat16)
    expert_out = lax.map(one_expert, (table, w_gate, w_up, w_down))
    flat_out = expert_out.reshape(EXPERTS * blocks * CAP, MODEL_DIMENSION)
    pick_index = (chosen * (blocks * CAP) + block_index * CAP + slot_rank).astype(jnp.int32)

    def one_block(operands):
        pick_row, weight_row = operands
        picked = jnp.take(flat_out, pick_row, axis=0).astype(jnp.float32)
        return lax.optimization_barrier(jnp.sum((picked * weight_row[:, None]).reshape(TOK_DEV, TOP, MODEL_DIMENSION), axis=1))
    moe_out = lax.map(one_block, (pick_index, route_weights.reshape(blocks, per_block)))
    final = mid.reshape(blocks * TOK_DEV, MODEL_DIMENSION).astype(jnp.float32) + moe_out.reshape(blocks * TOK_DEV, MODEL_DIMENSION)
    return final.astype(jnp.bfloat16).reshape(REQUEST_GROUPS, SUFFIX_LENGTH, MODEL_DIMENSION)
```

```python
import functools
import math

import jax
import jax.numpy as jnp
from jax import lax
from jax.experimental import pallas as pl
from jax.experimental.pallas import tpu as pltpu
from jax.sharding import PartitionSpec as P

ROPE_BASE = 500000.0
NORM_EPS = 1e-06
MASKED = -1e30
MESH = pl.DeviceIdType.MESH
Z, Y, X = 8, 4, 4
CHUNK_ORDER = (0, 1, 7, 2, 6, 3, 5, 4)
BACK = 2


class Copies:
    def __init__(self, send, recv):
        self.send, self.recv, self.made, self.open = send, recv, {}, []

    def start(self, key, src, dst, device):
        at = len(self.made)
        copy = pltpu.make_async_remote_copy(
            src_ref=src, dst_ref=dst, send_sem=self.send.at[at], recv_sem=self.recv.at[at],
            device_id=device, device_id_type=MESH,
        )
        copy.start()
        self.made[key] = copy
        self.open.append(key)

    def arrived(self, key):
        self.made[key].wait_recv()
        self.open.remove(key)

    def finish(self):
        for key in list(self.open):
            self.arrived(key)
        for copy in self.made.values():
            copy.wait_send()


def near(axis, step):
    if axis == "x":
        return {"head": lax.rem(lax.axis_index("head") + (step + X), X)}
    if axis == "core":
        return {"grp": 1 - lax.axis_index("grp")}
    tok = lax.axis_index("tok")
    z, y = tok // Y, lax.rem(tok, Y)
    if axis == "z":
        z = lax.rem(z + (step + Z), Z)
    else:
        y = lax.rem(y + (step + Y), Y)
    return {"tok": z * Y + y}


def greet(devices):
    barrier = pltpu.get_barrier_semaphore()
    for device in devices:
        pl.semaphore_signal(barrier, inc=1, device_id=device, device_id_type=MESH)
    pl.semaphore_wait(barrier, len(devices))


def torus_start(copies, kv, forward, backward):
    up, down = near("y", 1), near("y", -1)
    if forward:
        copies.start(("f", 1), kv.at[0, 0], kv.at[0, 1], near("z", 1))
    if backward:
        copies.start(("b", 1), kv.at[0, 0], kv.at[0, forward + backward], near("z", -1))
    copies.start(("u", 0), kv.at[0, 0], kv.at[1, 0], up)
    copies.start(("d", 0), kv.at[0, 0], kv.at[3, 0], down)


def torus_run(copies, kv, forward, backward):
    up, down = near("y", 1), near("y", -1)
    last = forward + backward
    for step in range(1, max(forward, backward) + 1):
        for mark, reach, slot, following, way in (
            ("f", forward, step, step + 1, 1),
            ("b", backward, last + 1 - step, last - step, -1),
        ):
            if step > reach:
                continue
            copies.arrived((mark, step))
            if step < reach:
                copies.start((mark, step + 1), kv.at[0, slot], kv.at[0, following], near("z", way))
            copies.start(("u", slot), kv.at[0, slot], kv.at[1, slot], up)
            copies.start(("d", slot), kv.at[0, slot], kv.at[3, slot], down)
    half = (last + 1) // 2
    for slot in range(last + 1):
        if slot <= half:
            copies.arrived(("u", slot))
            copies.start(("v", slot), kv.at[1, slot], kv.at[2, slot], up)
        else:
            copies.arrived(("d", slot))
            copies.start(("v", slot), kv.at[3, slot], kv.at[2, slot], down)


def torus_copies(forward, backward):
    slots = forward + backward + 1
    return forward + backward + 3 * slots


def ring_start(copies, key, ref, width, rows, offset):
    me = lax.axis_index("head")
    own = ref.at[pl.ds(offset, rows), pl.ds(pl.multiple_of(me * width, 128), width)]
    copies.start((key, "r"), own, own, near("x", 1))
    copies.start((key, "l"), own, own, near("x", -1))


def ring_relay(copies, key, ref, width, rows, offset):
    me = lax.axis_index("head")
    half = rows // 2
    copies.arrived((key, "r"))
    left = lax.rem(me + (X - 1), X)
    first = ref.at[pl.ds(offset, half), pl.ds(pl.multiple_of(left * width, 128), width)]
    copies.start((key, "rr"), first, first, near("x", 1))
    copies.arrived((key, "l"))
    right = lax.rem(me + 1, X)
    second = ref.at[pl.ds(offset + half, half), pl.ds(pl.multiple_of(right * width, 128), width)]
    copies.start((key, "ll"), second, second, near("x", -1))


def local(pairs, sems):
    made = [pltpu.make_async_copy(a, b, sems.at[i]) for i, (a, b) in enumerate(pairs)]
    for copy in made:
        copy.start()
    for copy in made:
        copy.wait()


VM = pl.BlockSpec(memory_space=pltpu.VMEM)
HB = pl.BlockSpec(memory_space=pl.ANY)


def call(kernel, ident, ins, outs, in_specs, out_specs, copies, extra=()):
    return pl.pallas_call(
        kernel,
        out_shape=outs,
        in_specs=in_specs,
        out_specs=out_specs,
        scratch_shapes=[
            pltpu.SemaphoreType.DMA((copies,)),
            pltpu.SemaphoreType.DMA((copies,)),
            pltpu.SemaphoreType.DMA((3,)),
            *extra,
        ],
        compiler_params=pltpu.CompilerParams(collective_id=ident, has_side_effects=True),
    )(*ins)


def shape(*dims, dtype=jnp.bfloat16):
    return jax.ShapeDtypeStruct(dims, dtype)


def prologue_kernel(hid, pk, pv, wq, wk, wv, wo, feat, kv, wq2, wk2, wv2, wo2, send, recv, sems):
    me = lax.axis_index("head")
    width = hid.shape[1]
    local(
        [
            (pk, kv.at[0, 0, 0]),
            (pv, kv.at[0, 0, 1]),
            (hid, feat.at[:, pl.ds(pl.multiple_of(me * width, 128), width)]),
        ],
        sems,
    )
    core = near("core", 1)
    greet([near("x", 1), near("x", -1), near("y", 1), near("y", -1), near("z", 1), near("z", -1), core])
    copies = Copies(send, recv)
    torus_start(copies, kv, 4, 3)
    ring_start(copies, "h", feat, width, hid.shape[0], 0)
    for key, a, b in (("q", wq, wq2), ("k", wk, wk2), ("w", wv, wv2), ("o", wo, wo2)):
        copies.start(key, a, b, core)
    torus_run(copies, kv, 4, 3)
    ring_relay(copies, "h", feat, width, hid.shape[0], 0)
    copies.finish()


def suffix_kernel(own, kv, send, recv, sems):
    local([(own, kv.at[0, 0])], sems)
    greet([near("y", 1), near("y", -1), near("z", 1), near("z", -1)])
    copies = Copies(send, recv)
    torus_start(copies, kv, BACK, 0)
    torus_run(copies, kv, BACK, 0)
    copies.finish()


def exchange_kernel(parts, got, send, recv, sems):
    me = lax.axis_index("head")
    greet([near("x", d) for d in range(1, X)])
    copies = Copies(send, recv)
    for d in (2, 1, 3):
        to = lax.rem(me + d, X)
        copies.start(d, parts.at[to], got.at[d - 1], near("x", d))
    copies.finish()


def small_kernel(block, got, send, recv, sems):
    greet([near("x", d) for d in range(1, X)])
    copies = Copies(send, recv)
    for d in (2, 1, 3):
        copies.start(d, block, got.at[d - 1], near("x", d))
    copies.finish()


def partner(slot, sign):
    tok = lax.axis_index("tok")
    grp = lax.axis_index("grp")
    dz, dy, dg = slot // 8, lax.rem(slot // 2, 4), lax.rem(slot, 2)
    z = lax.rem(tok // Y + Z + sign * dz, Z)
    y = lax.rem(lax.rem(tok, Y) + Y + sign * dy, Y)
    return {"grp": lax.rem(grp + dg, 2), "tok": z * Y + y}


def greet_all(more):
    barrier = pltpu.get_barrier_semaphore()

    def body(slot, carry):
        pl.semaphore_signal(barrier, inc=1, device_id=partner(slot, 1), device_id_type=MESH)
        return carry

    lax.fori_loop(1, 64, body, 0)
    for device in more:
        pl.semaphore_signal(barrier, inc=1, device_id=device, device_id_type=MESH)
    pl.semaphore_wait(barrier, 63 + len(more))


def dispatch_kernel(outgoing, rows, send, recv, sems, sent, came):
    me = lax.axis_index("head")
    width = outgoing.shape[1]
    cap = outgoing.shape[0] // 64
    columns = pl.ds(pl.multiple_of(me * width, 128), width)

    def copy_of(slot):
        at = pl.ds(pl.multiple_of(slot * cap, cap), cap)
        return pltpu.make_async_remote_copy(
            src_ref=outgoing.at[at, :], dst_ref=rows.at[at, columns],
            send_sem=sent.at[slot], recv_sem=came.at[slot],
            device_id=partner(slot, 1), device_id_type=MESH,
        )

    def start(slot, carry):
        copy_of(slot).start()
        return carry

    def wait_recv(slot, carry):
        copy_of(slot).wait_recv()
        return carry

    def wait_send(slot, carry):
        copy_of(slot).wait_send()
        return carry

    own = pltpu.make_async_copy(outgoing.at[pl.ds(0, cap), :], rows.at[pl.ds(0, cap), columns], sems.at[0])
    own.start()
    greet_all([near("x", 1), near("x", -1)])
    for chunk in CHUNK_ORDER:
        lax.fori_loop(max(8 * chunk, 1), 8 * chunk + 8, start, 0)
    own.wait()
    copies = Copies(send, recv)
    before = None
    for chunk in CHUNK_ORDER:
        lax.fori_loop(max(8 * chunk, 1), 8 * chunk + 8, wait_recv, 0)
        ring_start(copies, chunk, rows, width, 8 * cap, 8 * cap * chunk)
        if before is not None:
            ring_relay(copies, before, rows, width, 8 * cap, 8 * cap * before)
        before = chunk
    ring_relay(copies, before, rows, width, 8 * cap, 8 * cap * before)
    copies.finish()
    lax.fori_loop(1, 64, wait_send, 0)


def hidden_kernel(block, full, send, recv, sems):
    me = lax.axis_index("head")
    count, width = block.shape
    pieces = 4
    step = count // pieces
    own = pltpu.make_async_copy(
        block, full.at[:, pl.ds(pl.multiple_of(me * width, 128), width)], sems.at[0]
    )
    own.start()
    greet([near("x", 1), near("x", -1)])
    own.wait()
    copies = Copies(send, recv)
    for piece in range(pieces):
        ring_start(copies, piece, full, width, step, piece * step)
    for piece in range(pieces):
        ring_relay(copies, piece, full, width, step, piece * step)
    copies.finish()


def return_kernel(outputs, back, send, recv, sems, sent, came):
    cap = outputs.shape[0] // 64

    def copy_of(slot):
        at = pl.ds(pl.multiple_of(slot * cap, cap), cap)
        return pltpu.make_async_remote_copy(
            src_ref=outputs.at[at, :], dst_ref=back.at[at, :],
            send_sem=sent.at[slot], recv_sem=came.at[slot],
            device_id=partner(slot, -1), device_id_type=MESH,
        )

    def start(slot, carry):
        copy_of(slot).start()
        return carry

    def wait(slot, carry):
        copy_of(slot).wait()
        return carry

    own = pltpu.make_async_copy(outputs.at[pl.ds(0, cap), :], back.at[pl.ds(0, cap), :], sems.at[0])
    own.start()
    greet_all([])
    for chunk in CHUNK_ORDER:
        lax.fori_loop(max(8 * chunk, 1), 8 * chunk + 8, start, 0)
    own.wait()
    lax.fori_loop(1, 64, wait, 0)


def rms_norm(values_in, gain_vector):
    widened = values_in.astype(jnp.float32)
    mean_sq = jnp.mean(widened * widened, axis=-1, keepdims=True)
    return (widened * lax.rsqrt(mean_sq + NORM_EPS) * gain_vector.astype(jnp.float32)).astype(
        jnp.bfloat16
    )


def rotary_tables(token_positions, head_dim):
    half_dim = head_dim // 2
    frequency = jnp.exp(
        jnp.arange(half_dim, dtype=jnp.float32) * (-2.0 * math.log(ROPE_BASE) / head_dim)
    )
    angles = token_positions.astype(jnp.float32)[:, None] * frequency[None, :]
    return jnp.cos(angles), jnp.sin(angles)


def apply_rotary(product, cosine, sine_part):
    half_dim = product.shape[-1] // 2
    first_half = product[..., :half_dim]
    second_half = product[..., half_dim:]
    turned = jnp.concatenate(
        [
            first_half * cosine - second_half * sine_part,
            second_half * cosine + first_half * sine_part,
        ],
        axis=-1,
    )
    return turned.astype(jnp.bfloat16)


def attention_kernel(q, kv, sk, own_start, token_index, first, out):
    rows, dim = q.shape
    queries = q[...]
    scale = dim ** (-0.5)

    def step(state, keys, values, visible):
        top, total, summed = state
        scores = lax.dot_general(
            queries, keys, (((1,), (1,)), ((), ())), preferred_element_type=jnp.float32
        ) * scale
        if visible is not None:
            scores = jnp.where(visible, scores, MASKED)
        new_top = jnp.maximum(top, jnp.max(scores, axis=1, keepdims=True))
        weights = jnp.exp(scores - new_top)
        if visible is not None:
            weights = jnp.where(visible, weights, 0.0)
        factor = jnp.exp(top - new_top)
        total = total * factor + jnp.sum(weights, axis=1, keepdims=True)
        summed = summed * factor + jnp.dot(
            weights.astype(jnp.bfloat16), values, preferred_element_type=jnp.float32
        )
        return new_top, total, summed

    state = (
        jnp.full((rows, 1), MASKED, jnp.float32),
        jnp.zeros((rows, 1), jnp.float32),
        jnp.zeros((rows, dim), jnp.float32),
    )

    def prefix(index, state):
        return step(
            state,
            kv[index, :, 0].reshape(-1, dim),
            kv[index, :, 1].reshape(-1, dim),
            None,
        )

    state = lax.fori_loop(0, kv.shape[0], prefix, state)

    def suffix(index, state):
        keys = sk[index, :, 0].reshape(-1, dim)
        values = sk[index, :, 1].reshape(-1, dim)
        at = first[index, :][None, :]
        visible = (at >= own_start[...]) & (at <= token_index[...])
        return step(state, keys, values, visible)

    for index in range(sk.shape[0]):
        state = suffix(index, state)
    out[...] = (state[2] / state[1]).astype(out.dtype)


def on_device(
    hidden_in,
    attn_gain,
    w_query,
    key_projection_weight,
    value_projection_weight,
    w_out,
    prefix_keys,
    cached_prefix_values,
    request_lengths,
    moe_gain,
    expert_ids,
    route_weights,
    w_gate,
    w_up,
    w_down,
):
    f32, bf16 = jnp.float32, jnp.bfloat16
    tok_count = lax.axis_size("tok")
    tok_rank = lax.axis_index("tok")
    head_rank = lax.axis_index("head")
    grp_rank = lax.axis_index("grp")
    tok_dev = hidden_in.shape[1]
    model_width = attn_gain.shape[0]
    head_dim = prefix_keys.shape[3]
    prefix_dev = prefix_keys.shape[1]
    group_length = w_query.shape[1] // head_dim
    share = model_width // X
    quarter = hidden_in[0]

    features, prefix_kv, other_query, other_key, other_value, other_out = call(
        prologue_kernel, 0,
        (quarter, prefix_keys[0, :, 0], cached_prefix_values[0, :, 0], w_query,
         key_projection_weight, value_projection_weight, w_out),
        (shape(tok_dev, model_width), shape(Y, Z, 2, prefix_dev, head_dim), shape(*w_query.shape),
         shape(*key_projection_weight.shape), shape(*value_projection_weight.shape), shape(*w_out.shape)),
        [VM] * 3 + [HB] * 4, [VM] * 2 + [HB] * 4, torus_copies(4, 3) + 8,
    )
    attention_input = rms_norm(features, attn_gain)
    lengths = request_lengths[0]
    request_ends = jnp.cumsum(lengths)
    starts = request_ends - lengths
    token_index = tok_rank * tok_dev + jnp.arange(tok_dev, dtype=jnp.int32)
    own_start = jnp.max(
        jnp.where(starts[None, :] <= token_index[:, None], starts[None, :], 0), axis=1
    )
    token_positions = prefix_dev * tok_count + token_index - own_start
    cosine, sine_part = rotary_tables(token_positions, head_dim)

    half = model_width // 2
    lower = attention_input[:, :half]
    upper = attention_input[:, half:]
    mine = jnp.where(grp_rank == 0, lower, upper)
    others = jnp.where(grp_rank == 0, upper, lower)

    def project(own, other):
        return jnp.dot(mine, own, preferred_element_type=f32) + jnp.dot(
            others, other, preferred_element_type=f32
        )

    query_product = project(w_query, other_query).reshape(tok_dev, group_length, head_dim)
    key_product = project(key_projection_weight, other_key)
    value_product = project(value_projection_weight, other_value)
    queries = apply_rotary(
        jnp.transpose(query_product, (1, 0, 2)), cosine[None], sine_part[None]
    ).reshape(group_length * tok_dev, head_dim)
    suffix_own = jnp.stack(
        [apply_rotary(key_product, cosine, sine_part), value_product.astype(bf16)]
    )
    suffix_kv = call(
        suffix_kernel, 1, (suffix_own,), shape(Y, BACK + 1, 2, tok_dev, head_dim),
        [VM], VM, torus_copies(BACK, 0),
    )
    z_rank, y_rank = tok_rank // Y, tok_rank % Y
    y_from = (y_rank - jnp.arange(Y) + Y) % Y
    z_from = z_rank - jnp.arange(BACK + 1)
    device_from = jnp.where(z_from[None, :] >= 0, z_from[None, :] * Y + y_from[:, None], tok_count)
    key_index = (
        device_from[:, :, None] * tok_dev + jnp.arange(tok_dev, dtype=jnp.int32)
    ).reshape(Y, (BACK + 1) * tok_dev)
    rows = group_length * tok_dev
    attended = pl.pallas_call(
        attention_kernel,
        out_shape=shape(rows, head_dim),
        in_specs=[VM] * 6,
        out_specs=VM,
    )(
        queries, prefix_kv, suffix_kv,
        jnp.tile(own_start[:, None], (group_length, 1)),
        jnp.tile(token_index[:, None], (group_length, 1)),
        key_index.astype(jnp.int32),
    )
    attended = jnp.transpose(attended.reshape(group_length, tok_dev, head_dim), (1, 0, 2)).reshape(
        tok_dev, group_length * head_dim
    )

    def out_part(weights):
        return lax.dot_general(
            attended, weights, (((1,), (1,)), ((), ())), preferred_element_type=f32
        ).astype(bf16)

    own_part, other_part = out_part(w_out), out_part(other_out)
    first_part = jnp.where(grp_rank == 0, own_part, other_part)
    second_part = jnp.where(grp_rank == 0, other_part, own_part)
    parts = jnp.stack(
        [first_part[:, :share], first_part[:, share:], second_part[:, :share], second_part[:, share:]]
    )
    got = call(
        exchange_kernel, 2, (parts,), shape(X - 1, tok_dev, share), [VM], VM, X - 1
    )
    own_share = lax.dynamic_index_in_dim(parts, head_rank, 0, keepdims=False)
    mid = (
        quarter.astype(f32)
        + (own_share.astype(f32) + got[0].astype(f32) + got[1].astype(f32) + got[2].astype(f32))
    ).astype(bf16)
    mid_wide = mid.astype(f32)
    squares = jnp.sum(mid_wide * mid_wide, axis=1)
    small = jnp.broadcast_to(squares[None, :], (8, tok_dev))
    small_got = call(
        small_kernel, 3, (small,), shape(X - 1, 8, tok_dev, dtype=f32), [VM], VM, X - 1
    )
    mean_sq = (squares + small_got[0, 0] + small_got[1, 0] + small_got[2, 0]) / model_width
    gain = lax.dynamic_slice_in_dim(moe_gain, head_rank * share, share, 0).astype(f32)
    moe_in = (mid_wide * lax.rsqrt(mean_sq + NORM_EPS)[:, None] * gain).astype(bf16)

    experts = 2 * tok_count * w_gate.shape[0]
    top_count = expert_ids.shape[2]
    capacity = 4 * tok_dev * top_count // (3 * experts)
    chosen = expert_ids[0]
    e_grp, e_tok = chosen // tok_count, chosen % tok_count
    relative = (
        ((e_tok // Y - z_rank + Z) % Z) * 8
        + ((e_tok % Y - y_rank + Y) % Y) * 2
        + (e_grp + grp_rank) % 2
    )
    hit = relative[:, :, None] == jnp.arange(experts, dtype=jnp.int32)[None, None, :]
    uses = jnp.any(hit, axis=1)
    weight = jnp.sum(jnp.where(hit, route_weights[0][:, :, None], 0.0), axis=1)
    weight_hi = weight.astype(bf16)
    weight_lo = (weight - weight_hi.astype(f32)).astype(bf16)
    earlier = jnp.tril(jnp.ones((tok_dev, tok_dev), bf16), -1)
    rank = jnp.dot(earlier, uses.astype(bf16), preferred_element_type=f32)
    rank = jnp.where(uses, rank, -1.0).astype(bf16)
    slots = experts * capacity
    slot_index = jnp.arange(slots, dtype=jnp.int32)
    spread = (slot_index[None, :] // capacity == jnp.arange(experts, dtype=jnp.int32)[:, None]).astype(bf16)
    spread_rank = jnp.dot(rank, spread, preferred_element_type=f32)
    placed = spread_rank == (slot_index % capacity).astype(f32)[None, :]
    outgoing = lax.dot_general(
        placed.astype(bf16), moe_in, (((0,), (0,)), ((), ())), preferred_element_type=f32
    ).astype(bf16)

    flat_rows = call(
        dispatch_kernel, 4, (outgoing,), shape(slots, model_width), [VM], VM, 8 * 4,
        (pltpu.SemaphoreType.DMA((64,)), pltpu.SemaphoreType.DMA((64,))),
    )
    gate_act = jnp.dot(flat_rows, w_gate[0], preferred_element_type=f32)
    up_act = jnp.dot(flat_rows, w_up[0], preferred_element_type=f32)
    hidden = (jax.nn.silu(gate_act) * up_act).astype(bf16)
    full_hidden = call(
        hidden_kernel, 5, (hidden,), shape(slots, X * hidden.shape[1]), [VM], VM, 4 * 4
    )
    expert_out = jnp.dot(full_hidden, w_down[0], preferred_element_type=f32).astype(bf16)
    returned = call(
        return_kernel, 6, (expert_out,), shape(slots, share), [VM], VM, 1,
        (pltpu.SemaphoreType.DMA((64,)), pltpu.SemaphoreType.DMA((64,))),
    )

    def combine(part):
        spread_weight = jnp.where(placed, jnp.dot(part, spread, preferred_element_type=f32), 0.0)
        return jnp.dot(spread_weight.astype(bf16), returned, preferred_element_type=f32)

    output = (mid_wide + (combine(weight_hi) + combine(weight_lo))).astype(bf16)
    return output[None]


def solution(mesh):
    return jax.shard_map(
        on_device,
        mesh=mesh,
        in_specs=(
            P("grp", "tok", "head"),
            P(),
            P("grp", "head"),
            P("grp", "head"),
            P("grp", "head"),
            P("grp", "head"),
            P("grp", "tok", "head", None),
            P("grp", "tok", "head", None),
            P("grp", None),
            P(),
            P("grp", "tok", None),
            P("grp", "tok", None),
            P(("grp", "tok"), None, "head"),
            P(("grp", "tok"), None, "head"),
            P(("grp", "tok"), None, "head"),
        ),
        out_specs=P("grp", "tok", "head"),
        check_vma=False,
    )
```

```python
import functools
import math

import jax
import jax.numpy as jnp
from jax import lax
from jax.experimental import pallas as pl
from jax.experimental.pallas import tpu as pltpu
from jax.sharding import PartitionSpec as P

ROPE_BASE = 500000.0
NORM_EPS = 1e-06
MASKED = -1e30
MESH = pl.DeviceIdType.MESH
Z, Y, X = 8, 4, 4
CHUNK_ORDER = (0, 1, 5, 3, 4, 6, 2, 7)
BACK = 2


class Copies:
    def __init__(self, send, recv):
        self.send, self.recv, self.made, self.open = send, recv, {}, []

    def start(self, key, src, dst, device):
        at = len(self.made)
        copy = pltpu.make_async_remote_copy(
            src_ref=src, dst_ref=dst, send_sem=self.send.at[at], recv_sem=self.recv.at[at],
            device_id=device, device_id_type=MESH,
        )
        copy.start()
        self.made[key] = copy
        self.open.append(key)

    def arrived(self, key):
        self.made[key].wait_recv()
        self.open.remove(key)

    def finish(self):
        for key in list(self.open):
            self.arrived(key)
        for copy in self.made.values():
            copy.wait_send()


def near(axis, step):
    if axis == "x":
        return {"head": lax.rem(lax.axis_index("head") + (step + X), X)}
    if axis == "core":
        return {"grp": 1 - lax.axis_index("grp")}
    tok = lax.axis_index("tok")
    z, y = tok // Y, lax.rem(tok, Y)
    if axis == "z":
        z = lax.rem(z + (step + Z), Z)
    else:
        y = lax.rem(y + (step + Y), Y)
    return {"tok": z * Y + y}


def greet(devices):
    barrier = pltpu.get_barrier_semaphore()
    for device in devices:
        pl.semaphore_signal(barrier, inc=1, device_id=device, device_id_type=MESH)
    pl.semaphore_wait(barrier, len(devices))


def torus_start(copies, kv, forward, backward):
    up, down = near("y", 1), near("y", -1)
    if forward:
        copies.start(("f", 1), kv.at[0, 0], kv.at[0, 1], near("z", 1))
    if backward:
        copies.start(("b", 1), kv.at[0, 0], kv.at[0, forward + backward], near("z", -1))
    copies.start(("u", 0), kv.at[0, 0], kv.at[1, 0], up)
    copies.start(("d", 0), kv.at[0, 0], kv.at[3, 0], down)


def torus_run(copies, kv, forward, backward):
    up, down = near("y", 1), near("y", -1)
    last = forward + backward
    for step in range(1, max(forward, backward) + 1):
        for mark, reach, slot, following, way in (
            ("f", forward, step, step + 1, 1),
            ("b", backward, last + 1 - step, last - step, -1),
        ):
            if step > reach:
                continue
            copies.arrived((mark, step))
            if step < reach:
                copies.start((mark, step + 1), kv.at[0, slot], kv.at[0, following], near("z", way))
            copies.start(("u", slot), kv.at[0, slot], kv.at[1, slot], up)
            copies.start(("d", slot), kv.at[0, slot], kv.at[3, slot], down)
    half = (last + 1) // 2
    for slot in range(last + 1):
        if slot <= half:
            copies.arrived(("u", slot))
            copies.start(("v", slot), kv.at[1, slot], kv.at[2, slot], up)
        else:
            copies.arrived(("d", slot))
            copies.start(("v", slot), kv.at[3, slot], kv.at[2, slot], down)


def torus_copies(forward, backward):
    slots = forward + backward + 1
    return forward + backward + 3 * slots


def ring_start(copies, key, ref, width, rows, offset):
    me = lax.axis_index("head")
    own = ref.at[pl.ds(offset, rows), pl.ds(pl.multiple_of(me * width, 128), width)]
    copies.start((key, "r"), own, own, near("x", 1))
    copies.start((key, "l"), own, own, near("x", -1))


def ring_relay(copies, key, ref, width, rows, offset):
    me = lax.axis_index("head")
    half = rows // 2
    copies.arrived((key, "r"))
    left = lax.rem(me + (X - 1), X)
    first = ref.at[pl.ds(offset, half), pl.ds(pl.multiple_of(left * width, 128), width)]
    copies.start((key, "rr"), first, first, near("x", 1))
    copies.arrived((key, "l"))
    right = lax.rem(me + 1, X)
    second = ref.at[pl.ds(offset + half, half), pl.ds(pl.multiple_of(right * width, 128), width)]
    copies.start((key, "ll"), second, second, near("x", -1))


def local(pairs, sems):
    made = [pltpu.make_async_copy(a, b, sems.at[i]) for i, (a, b) in enumerate(pairs)]
    for copy in made:
        copy.start()
    for copy in made:
        copy.wait()


VM = pl.BlockSpec(memory_space=pltpu.VMEM)
HB = pl.BlockSpec(memory_space=pl.ANY)


def call(kernel, ident, ins, outs, in_specs, out_specs, copies, extra=()):
    return pl.pallas_call(
        kernel,
        out_shape=outs,
        in_specs=in_specs,
        out_specs=out_specs,
        scratch_shapes=[
            pltpu.SemaphoreType.DMA((copies,)),
            pltpu.SemaphoreType.DMA((copies,)),
            pltpu.SemaphoreType.DMA((4,)),
            *extra,
        ],
        compiler_params=pltpu.CompilerParams(collective_id=ident, has_side_effects=True),
    )(*ins)


def shape(*dims, dtype=jnp.bfloat16):
    return jax.ShapeDtypeStruct(dims, dtype)


def prologue_kernel(hid, pk, pv, wq, wk, wv, wo, feat, kv, wq2, wk2, wv2, wo2, send, recv, sems):
    me = lax.axis_index("head")
    width = hid.shape[1]
    local(
        [
            (pk, kv.at[0, 0, 0]),
            (pv, kv.at[0, 0, 1]),
            (hid, feat.at[:, pl.ds(pl.multiple_of(me * width, 128), width)]),
        ],
        sems,
    )
    core = near("core", 1)
    greet([near("x", 1), near("x", -1), near("y", 1), near("y", -1), near("z", 1), near("z", -1), core])
    copies = Copies(send, recv)
    torus_start(copies, kv, 4, 3)
    ring_start(copies, "h", feat, width, hid.shape[0], 0)
    for key, a, b in (("q", wq, wq2), ("k", wk, wk2), ("w", wv, wv2), ("o", wo, wo2)):
        copies.start(key, a, b, core)
    torus_run(copies, kv, 4, 3)
    ring_relay(copies, "h", feat, width, hid.shape[0], 0)
    copies.finish()


def suffix_kernel(own, kv, send, recv, sems):
    local([(own, kv.at[0, 0])], sems)
    greet([near("y", 1), near("y", -1), near("z", 1), near("z", -1)])
    copies = Copies(send, recv)
    torus_start(copies, kv, BACK, 0)
    torus_run(copies, kv, BACK, 0)
    copies.finish()


def exchange_kernel(parts, got, send, recv, sems):
    me = lax.axis_index("head")
    greet([near("x", d) for d in range(1, X)])
    copies = Copies(send, recv)
    for d in (2, 1, 3):
        to = lax.rem(me + d, X)
        copies.start(d, parts.at[to], got.at[d - 1], near("x", d))
    copies.finish()


def small_kernel(block, got, send, recv, sems):
    greet([near("x", d) for d in range(1, X)])
    copies = Copies(send, recv)
    for d in (2, 1, 3):
        copies.start(d, block, got.at[d - 1], near("x", d))
    copies.finish()


def partner(slot, sign):
    tok = lax.axis_index("tok")
    grp = lax.axis_index("grp")
    dz, dy, dg = slot // 8, lax.rem(slot // 2, 4), lax.rem(slot, 2)
    z = lax.rem(tok // Y + Z + sign * dz, Z)
    y = lax.rem(lax.rem(tok, Y) + Y + sign * dy, Y)
    return {"grp": lax.rem(grp + dg, 2), "tok": z * Y + y}


def greet_all(more):
    barrier = pltpu.get_barrier_semaphore()

    def body(slot, carry):
        pl.semaphore_signal(barrier, inc=1, device_id=partner(slot, 1), device_id_type=MESH)
        return carry

    lax.fori_loop(1, 64, body, 0)
    for device in more:
        pl.semaphore_signal(barrier, inc=1, device_id=device, device_id_type=MESH)
    pl.semaphore_wait(barrier, 63 + len(more))


def experts_kernel(
    outgoing, w_gate, w_up, w_down, back,
    send, recv, sems, sent, came, sent_back, came_back, rows, hidden, results, wide, down,
):
    me = lax.axis_index("head")
    width = outgoing.shape[1]
    cap = outgoing.shape[0] // 64
    inner = w_gate.shape[1]
    many = 8 * cap
    columns = pl.ds(pl.multiple_of(me * width, 128), width)
    own_hidden = pl.ds(pl.multiple_of(me * inner, 128), inner)

    def block(slot):
        return pl.ds(pl.multiple_of(slot * cap, cap), cap)

    def there(slot):
        return pltpu.make_async_remote_copy(
            src_ref=outgoing.at[block(slot), :], dst_ref=rows.at[block(slot), columns],
            send_sem=sent.at[slot], recv_sem=came.at[slot],
            device_id=partner(slot, 1), device_id_type=MESH,
        )

    def home(slot):
        return pltpu.make_async_remote_copy(
            src_ref=results.at[block(slot), :], dst_ref=back.at[block(slot), :],
            send_sem=sent_back.at[slot], recv_sem=came_back.at[slot],
            device_id=partner(slot, -1), device_id_type=MESH,
        )

    def each(first, last, act):
        def body(slot, carry):
            act(slot)
            return carry

        lax.fori_loop(first, last, body, 0)

    def of_chunk(chunk, act):
        each(max(8 * chunk, 1), 8 * chunk + 8, act)

    weights = [
        pltpu.make_async_copy(w_gate, wide.at[:, pl.ds(0, inner)], sems.at[0]),
        pltpu.make_async_copy(w_up, wide.at[:, pl.ds(inner, inner)], sems.at[1]),
        pltpu.make_async_copy(w_down, down, sems.at[2]),
    ]
    own = pltpu.make_async_copy(outgoing.at[block(0), :], rows.at[block(0), columns], sems.at[3])
    own.start()
    for copy in weights:
        copy.start()
    greet_all([near("x", 1), near("x", -1)])
    for chunk in CHUNK_ORDER:
        of_chunk(chunk, lambda slot: there(slot).start())
    own.wait()
    for copy in weights:
        copy.wait()
    copies = Copies(send, recv)
    last = pltpu.make_async_copy(results.at[block(0), :], back.at[block(0), :], sems.at[3])

    def arrive(chunk):
        of_chunk(chunk, lambda slot: there(slot).wait_recv())
        ring_start(copies, ("m", chunk), rows, width, many, many * chunk)

    def pass_rows(chunk):
        ring_relay(copies, ("m", chunk), rows, width, many, many * chunk)

    def gate_up(chunk):
        copies.arrived((("m", chunk), "rr"))
        copies.arrived((("m", chunk), "ll"))
        at = pl.ds(many * chunk, many)
        both = jnp.dot(rows[at, :], wide[...], preferred_element_type=jnp.float32)
        gate = both[:, :inner]
        hidden[at, own_hidden] = (gate / (1.0 + jnp.exp(-gate)) * both[:, inner:]).astype(hidden.dtype)

    def send_hidden(chunk):
        of_chunk(chunk, lambda slot: there(slot).wait_send())
        ring_start(copies, ("h", chunk), hidden, inner, many, many * chunk)

    def pass_hidden(chunk):
        ring_relay(copies, ("h", chunk), hidden, inner, many, many * chunk)

    def finish(chunk):
        copies.arrived((("h", chunk), "rr"))
        copies.arrived((("h", chunk), "ll"))
        at = pl.ds(many * chunk, many)
        results[at, :] = jnp.dot(
            hidden[at, :], down[...], preferred_element_type=jnp.float32
        ).astype(results.dtype)

    def send_home(chunk):
        if chunk == 0:
            last.start()
        of_chunk(chunk, lambda slot: home(slot).start())

    stages = ((arrive, 0), (pass_rows, 1), (gate_up, 2), (pass_hidden, 3), (send_hidden, 2), (send_home, 5), (finish, 4))
    for step in range(len(CHUNK_ORDER) + 5):
        for stage, lag in stages:
            if 0 <= step - lag < len(CHUNK_ORDER):
                stage(CHUNK_ORDER[step - lag])
    copies.finish()
    last.wait()
    each(1, 64, lambda slot: home(slot).wait())


def rms_norm(values_in, gain_vector):
    widened = values_in.astype(jnp.float32)
    mean_sq = jnp.mean(widened * widened, axis=-1, keepdims=True)
    return (widened * lax.rsqrt(mean_sq + NORM_EPS) * gain_vector.astype(jnp.float32)).astype(
        jnp.bfloat16
    )


def rotary_tables(token_positions, head_dim):
    half_dim = head_dim // 2
    frequency = jnp.exp(
        jnp.arange(half_dim, dtype=jnp.float32) * (-2.0 * math.log(ROPE_BASE) / head_dim)
    )
    angles = token_positions.astype(jnp.float32)[:, None] * frequency[None, :]
    return jnp.cos(angles), jnp.sin(angles)


def apply_rotary(product, cosine, sine_part):
    half_dim = product.shape[-1] // 2
    first_half = product[..., :half_dim]
    second_half = product[..., half_dim:]
    turned = jnp.concatenate(
        [
            first_half * cosine - second_half * sine_part,
            second_half * cosine + first_half * sine_part,
        ],
        axis=-1,
    )
    return turned.astype(jnp.bfloat16)


def attention_kernel(q, kv, sk, own_start, token_index, first, out):
    rows, dim = q.shape
    queries = q[...]
    scale = dim ** (-0.5)

    def step(state, keys, values, visible):
        top, total, summed = state
        scores = lax.dot_general(
            queries, keys, (((1,), (1,)), ((), ())), preferred_element_type=jnp.float32
        ) * scale
        if visible is not None:
            scores = jnp.where(visible, scores, MASKED)
        new_top = jnp.maximum(top, jnp.max(scores, axis=1, keepdims=True))
        weights = jnp.exp(scores - new_top)
        if visible is not None:
            weights = jnp.where(visible, weights, 0.0)
        factor = jnp.exp(top - new_top)
        total = total * factor + jnp.sum(weights, axis=1, keepdims=True)
        summed = summed * factor + jnp.dot(
            weights.astype(jnp.bfloat16), values, preferred_element_type=jnp.float32
        )
        return new_top, total, summed

    state = (
        jnp.full((rows, 1), MASKED, jnp.float32),
        jnp.zeros((rows, 1), jnp.float32),
        jnp.zeros((rows, dim), jnp.float32),
    )

    def prefix(index, state):
        return step(
            state,
            kv[index, :, 0].reshape(-1, dim),
            kv[index, :, 1].reshape(-1, dim),
            None,
        )

    state = lax.fori_loop(0, kv.shape[0], prefix, state)

    def suffix(index, state):
        keys = sk[index, :, 0].reshape(-1, dim)
        values = sk[index, :, 1].reshape(-1, dim)
        at = first[index, :][None, :]
        visible = (at >= own_start[...]) & (at <= token_index[...])
        return step(state, keys, values, visible)

    for index in range(sk.shape[0]):
        state = suffix(index, state)
    out[...] = (state[2] / state[1]).astype(out.dtype)


def on_device(
    hidden_in,
    attn_gain,
    w_query,
    key_projection_weight,
    value_projection_weight,
    w_out,
    prefix_keys,
    cached_prefix_values,
    request_lengths,
    moe_gain,
    expert_ids,
    route_weights,
    w_gate,
    w_up,
    w_down,
):
    f32, bf16 = jnp.float32, jnp.bfloat16
    tok_count = lax.axis_size("tok")
    tok_rank = lax.axis_index("tok")
    head_rank = lax.axis_index("head")
    grp_rank = lax.axis_index("grp")
    tok_dev = hidden_in.shape[1]
    model_width = attn_gain.shape[0]
    head_dim = prefix_keys.shape[3]
    prefix_dev = prefix_keys.shape[1]
    group_length = w_query.shape[1] // head_dim
    share = model_width // X
    quarter = hidden_in[0]

    features, prefix_kv, other_query, other_key, other_value, other_out = call(
        prologue_kernel, 0,
        (quarter, prefix_keys[0, :, 0], cached_prefix_values[0, :, 0], w_query,
         key_projection_weight, value_projection_weight, w_out),
        (shape(tok_dev, model_width), shape(Y, Z, 2, prefix_dev, head_dim), shape(*w_query.shape),
         shape(*key_projection_weight.shape), shape(*value_projection_weight.shape), shape(*w_out.shape)),
        [VM] * 3 + [HB] * 4, [VM] * 2 + [HB] * 4, torus_copies(4, 3) + 8,
    )
    attention_input = rms_norm(features, attn_gain)
    lengths = request_lengths[0]
    request_ends = jnp.cumsum(lengths)
    starts = request_ends - lengths
    token_index = tok_rank * tok_dev + jnp.arange(tok_dev, dtype=jnp.int32)
    own_start = jnp.max(
        jnp.where(starts[None, :] <= token_index[:, None], starts[None, :], 0), axis=1
    )
    token_positions = prefix_dev * tok_count + token_index - own_start
    cosine, sine_part = rotary_tables(token_positions, head_dim)

    half = model_width // 2
    lower = attention_input[:, :half]
    upper = attention_input[:, half:]
    mine = jnp.where(grp_rank == 0, lower, upper)
    others = jnp.where(grp_rank == 0, upper, lower)

    def project(own, other):
        return jnp.dot(mine, own, preferred_element_type=f32) + jnp.dot(
            others, other, preferred_element_type=f32
        )

    query_product = project(w_query, other_query).reshape(tok_dev, group_length, head_dim)
    key_product = project(key_projection_weight, other_key)
    value_product = project(value_projection_weight, other_value)
    queries = apply_rotary(
        jnp.transpose(query_product, (1, 0, 2)), cosine[None], sine_part[None]
    ).reshape(group_length * tok_dev, head_dim)
    suffix_own = jnp.stack(
        [apply_rotary(key_product, cosine, sine_part), value_product.astype(bf16)]
    )
    suffix_kv = call(
        suffix_kernel, 1, (suffix_own,), shape(Y, BACK + 1, 2, tok_dev, head_dim),
        [VM], VM, torus_copies(BACK, 0),
    )
    z_rank, y_rank = tok_rank // Y, tok_rank % Y
    y_from = (y_rank - jnp.arange(Y) + Y) % Y
    z_from = z_rank - jnp.arange(BACK + 1)
    device_from = jnp.where(z_from[None, :] >= 0, z_from[None, :] * Y + y_from[:, None], tok_count)
    key_index = (
        device_from[:, :, None] * tok_dev + jnp.arange(tok_dev, dtype=jnp.int32)
    ).reshape(Y, (BACK + 1) * tok_dev)
    rows = group_length * tok_dev
    attended = pl.pallas_call(
        attention_kernel,
        out_shape=shape(rows, head_dim),
        in_specs=[VM] * 6,
        out_specs=VM,
    )(
        queries, prefix_kv, suffix_kv,
        jnp.tile(own_start[:, None], (group_length, 1)),
        jnp.tile(token_index[:, None], (group_length, 1)),
        key_index.astype(jnp.int32),
    )
    attended = jnp.transpose(attended.reshape(group_length, tok_dev, head_dim), (1, 0, 2)).reshape(
        tok_dev, group_length * head_dim
    )

    def out_part(weights):
        return lax.dot_general(
            attended, weights, (((1,), (1,)), ((), ())), preferred_element_type=f32
        ).astype(bf16)

    own_part, other_part = out_part(w_out), out_part(other_out)
    first_part = jnp.where(grp_rank == 0, own_part, other_part)
    second_part = jnp.where(grp_rank == 0, other_part, own_part)
    parts = jnp.stack(
        [first_part[:, :share], first_part[:, share:], second_part[:, :share], second_part[:, share:]]
    )
    got = call(
        exchange_kernel, 2, (parts,), shape(X - 1, tok_dev, share), [VM], VM, X - 1
    )
    own_share = lax.dynamic_index_in_dim(parts, head_rank, 0, keepdims=False)
    mid = (
        quarter.astype(f32)
        + (own_share.astype(f32) + got[0].astype(f32) + got[1].astype(f32) + got[2].astype(f32))
    ).astype(bf16)
    mid_wide = mid.astype(f32)
    squares = jnp.sum(mid_wide * mid_wide, axis=1)
    small = jnp.broadcast_to(squares[None, :], (8, tok_dev))
    small_got = call(
        small_kernel, 3, (small,), shape(X - 1, 8, tok_dev, dtype=f32), [VM], VM, X - 1
    )
    mean_sq = (squares + small_got[0, 0] + small_got[1, 0] + small_got[2, 0]) / model_width
    gain = lax.dynamic_slice_in_dim(moe_gain, head_rank * share, share, 0).astype(f32)
    moe_in = (mid_wide * lax.rsqrt(mean_sq + NORM_EPS)[:, None] * gain).astype(bf16)

    experts = 2 * tok_count * w_gate.shape[0]
    top_count = expert_ids.shape[2]
    capacity = 4 * tok_dev * top_count // (3 * experts)
    chosen = expert_ids[0]
    e_grp, e_tok = chosen // tok_count, chosen % tok_count
    relative = (
        ((e_tok // Y - z_rank + Z) % Z) * 8
        + ((e_tok % Y - y_rank + Y) % Y) * 2
        + (e_grp + grp_rank) % 2
    )
    hit = relative[:, :, None] == jnp.arange(experts, dtype=jnp.int32)[None, None, :]
    uses = jnp.any(hit, axis=1)
    weight = jnp.sum(jnp.where(hit, route_weights[0][:, :, None], 0.0), axis=1)
    weight_hi = weight.astype(bf16)
    weight_lo = (weight - weight_hi.astype(f32)).astype(bf16)
    earlier = jnp.tril(jnp.ones((tok_dev, tok_dev), bf16), -1)
    rank = jnp.dot(earlier, uses.astype(bf16), preferred_element_type=f32)
    rank = jnp.where(uses, rank, -1.0).astype(bf16)
    slots = experts * capacity
    slot_index = jnp.arange(slots, dtype=jnp.int32)
    spread = (slot_index[None, :] // capacity == jnp.arange(experts, dtype=jnp.int32)[:, None]).astype(bf16)
    spread_rank = jnp.dot(rank, spread, preferred_element_type=f32)
    placed = spread_rank == (slot_index % capacity).astype(f32)[None, :]
    outgoing = lax.dot_general(
        placed.astype(bf16), moe_in, (((0,), (0,)), ((), ())), preferred_element_type=f32
    ).astype(bf16)

    inner = w_gate.shape[2]
    returned = call(
        experts_kernel, 4, (outgoing, w_gate[0], w_up[0], w_down[0]), shape(slots, share),
        [VM] + [HB] * 3, VM, 2 * 8 * 4,
        (
            *[pltpu.SemaphoreType.DMA((64,))] * 4,
            pltpu.VMEM((slots, model_width), bf16),
            pltpu.VMEM((slots, X * inner), bf16),
            pltpu.VMEM((slots, share), bf16),
            pltpu.VMEM((model_width, 2 * inner), bf16),
            pltpu.VMEM((X * inner, share), bf16),
        ),
    )

    def combine(part):
        spread_weight = jnp.where(placed, jnp.dot(part, spread, preferred_element_type=f32), 0.0)
        return jnp.dot(spread_weight.astype(bf16), returned, preferred_element_type=f32)

    output = (mid_wide + (combine(weight_hi) + combine(weight_lo))).astype(bf16)
    return output[None]


def solution(mesh):
    return jax.shard_map(
        on_device,
        mesh=mesh,
        in_specs=(
            P("grp", "tok", "head"),
            P(),
            P("grp", "head"),
            P("grp", "head"),
            P("grp", "head"),
            P("grp", "head"),
            P("grp", "tok", "head", None),
            P("grp", "tok", "head", None),
            P("grp", None),
            P(),
            P("grp", "tok", None),
            P("grp", "tok", None),
            P(("grp", "tok"), None, "head"),
            P(("grp", "tok"), None, "head"),
            P(("grp", "tok"), None, "head"),
        ),
        out_specs=P("grp", "tok", "head"),
        check_vma=False,
    )
```

```python
import functools
import math

import jax
import jax.numpy as jnp
from jax import lax
from jax.experimental import pallas as pl
from jax.experimental.pallas import tpu as pltpu
from jax.sharding import PartitionSpec as P

ROPE_BASE = 500000.0
NORM_EPS = 1e-06
MASKED = -1e30
MESH = pl.DeviceIdType.MESH
Z, Y, X = 8, 4, 4
CHUNK_ORDER = (0, 1, 5, 3, 4, 6, 2, 7)
BACK = 2


class Copies:
    def __init__(self, send, recv):
        self.send, self.recv, self.made, self.open = send, recv, {}, []

    def start(self, key, src, dst, device):
        at = len(self.made)
        copy = pltpu.make_async_remote_copy(
            src_ref=src, dst_ref=dst, send_sem=self.send.at[at], recv_sem=self.recv.at[at],
            device_id=device, device_id_type=MESH,
        )
        copy.start()
        self.made[key] = copy
        self.open.append(key)

    def arrived(self, key):
        self.made[key].wait_recv()
        self.open.remove(key)

    def finish(self):
        for key in list(self.open):
            self.arrived(key)
        for copy in self.made.values():
            copy.wait_send()


def near(axis, step):
    if axis == "x":
        return {"head": lax.rem(lax.axis_index("head") + (step + X), X)}
    if axis == "core":
        return {"grp": 1 - lax.axis_index("grp")}
    tok = lax.axis_index("tok")
    z, y = tok // Y, lax.rem(tok, Y)
    if axis == "z":
        z = lax.rem(z + (step + Z), Z)
    else:
        y = lax.rem(y + (step + Y), Y)
    return {"tok": z * Y + y}


def greet(devices):
    barrier = pltpu.get_barrier_semaphore()
    for device in devices:
        pl.semaphore_signal(barrier, inc=1, device_id=device, device_id_type=MESH)
    pl.semaphore_wait(barrier, len(devices))


def torus_start(copies, kv, forward, backward):
    up, down = near("y", 1), near("y", -1)
    if forward:
        copies.start(("f", 1), kv.at[0, 0], kv.at[0, 1], near("z", 1))
    if backward:
        copies.start(("b", 1), kv.at[0, 0], kv.at[0, forward + backward], near("z", -1))
    copies.start(("u", 0), kv.at[0, 0], kv.at[1, 0], up)
    copies.start(("d", 0), kv.at[0, 0], kv.at[3, 0], down)


def torus_run(copies, kv, forward, backward):
    up, down = near("y", 1), near("y", -1)
    last = forward + backward
    for step in range(1, max(forward, backward) + 1):
        for mark, reach, slot, following, way in (
            ("f", forward, step, step + 1, 1),
            ("b", backward, last + 1 - step, last - step, -1),
        ):
            if step > reach:
                continue
            copies.arrived((mark, step))
            if step < reach:
                copies.start((mark, step + 1), kv.at[0, slot], kv.at[0, following], near("z", way))
            copies.start(("u", slot), kv.at[0, slot], kv.at[1, slot], up)
            copies.start(("d", slot), kv.at[0, slot], kv.at[3, slot], down)
    half = (last + 1) // 2
    for slot in range(last + 1):
        if slot <= half:
            copies.arrived(("u", slot))
            copies.start(("v", slot), kv.at[1, slot], kv.at[2, slot], up)
        else:
            copies.arrived(("d", slot))
            copies.start(("v", slot), kv.at[3, slot], kv.at[2, slot], down)


def torus_copies(forward, backward):
    slots = forward + backward + 1
    return forward + backward + 3 * slots


def ring_start(copies, key, ref, width, rows, offset):
    me = lax.axis_index("head")
    own = ref.at[pl.ds(offset, rows), pl.ds(pl.multiple_of(me * width, 128), width)]
    copies.start((key, "r"), own, own, near("x", 1))
    copies.start((key, "l"), own, own, near("x", -1))


def ring_relay(copies, key, ref, width, rows, offset):
    me = lax.axis_index("head")
    half = rows // 2
    copies.arrived((key, "r"))
    left = lax.rem(me + (X - 1), X)
    first = ref.at[pl.ds(offset, half), pl.ds(pl.multiple_of(left * width, 128), width)]
    copies.start((key, "rr"), first, first, near("x", 1))
    copies.arrived((key, "l"))
    right = lax.rem(me + 1, X)
    second = ref.at[pl.ds(offset + half, half), pl.ds(pl.multiple_of(right * width, 128), width)]
    copies.start((key, "ll"), second, second, near("x", -1))


def local(pairs, sems):
    made = [pltpu.make_async_copy(a, b, sems.at[i]) for i, (a, b) in enumerate(pairs)]
    for copy in made:
        copy.start()
    for copy in made:
        copy.wait()


VM = pl.BlockSpec(memory_space=pltpu.VMEM)
HB = pl.BlockSpec(memory_space=pl.ANY)


def call(kernel, ident, ins, outs, in_specs, out_specs, copies, extra=()):
    return pl.pallas_call(
        kernel,
        out_shape=outs,
        in_specs=in_specs,
        out_specs=out_specs,
        scratch_shapes=[
            pltpu.SemaphoreType.DMA((copies,)),
            pltpu.SemaphoreType.DMA((copies,)),
            pltpu.SemaphoreType.DMA((4,)),
            *extra,
        ],
        compiler_params=pltpu.CompilerParams(collective_id=ident, has_side_effects=True),
    )(*ins)


def shape(*dims, dtype=jnp.bfloat16):
    return jax.ShapeDtypeStruct(dims, dtype)


def prologue_kernel(hid, pk, pv, wq, wk, wv, wo, feat, kv, wq2, wk2, wv2, wo2, send, recv, sems):
    me = lax.axis_index("head")
    width = hid.shape[1]
    local(
        [
            (pk, kv.at[0, 0, 0]),
            (pv, kv.at[0, 0, 1]),
            (hid, feat.at[:, pl.ds(pl.multiple_of(me * width, 128), width)]),
        ],
        sems,
    )
    core = near("core", 1)
    greet([near("x", 1), near("x", -1), near("y", 1), near("y", -1), near("z", 1), near("z", -1), core])
    copies = Copies(send, recv)
    torus_start(copies, kv, 4, 3)
    ring_start(copies, "h", feat, width, hid.shape[0], 0)
    for key, a, b in (("q", wq, wq2), ("k", wk, wk2), ("w", wv, wv2), ("o", wo, wo2)):
        copies.start(key, a, b, core)
    torus_run(copies, kv, 4, 3)
    ring_relay(copies, "h", feat, width, hid.shape[0], 0)
    copies.finish()


def exchange_kernel(parts, got, send, recv, sems, transit):
    me = lax.axis_index("head")
    half = parts.shape[1] // 2
    greet([near("x", 1), near("x", -1)])
    copies = Copies(send, recv)
    right, left, opposite = (lax.rem(me + d, X) for d in (1, 3, 2))
    copies.start("tr", parts.at[opposite, pl.ds(0, half)], transit.at[0], near("x", 1))
    copies.start("tl", parts.at[opposite, pl.ds(half, half)], transit.at[1], near("x", -1))
    copies.start("r", parts.at[right], got.at[0], near("x", 1))
    copies.start("l", parts.at[left], got.at[2], near("x", -1))
    copies.arrived("tr")
    copies.start("rr", transit.at[0], got.at[1, pl.ds(0, half)], near("x", 1))
    copies.arrived("tl")
    copies.start("ll", transit.at[1], got.at[1, pl.ds(half, half)], near("x", -1))
    copies.finish()


def partner(slot, sign):
    tok = lax.axis_index("tok")
    grp = lax.axis_index("grp")
    dz, dy, dg = slot // 8, lax.rem(slot // 2, 4), lax.rem(slot, 2)
    z = lax.rem(tok // Y + Z + sign * dz, Z)
    y = lax.rem(lax.rem(tok, Y) + Y + sign * dy, Y)
    return {"grp": lax.rem(grp + dg, 2), "tok": z * Y + y}


def greet_all(more):
    barrier = pltpu.get_barrier_semaphore()

    def body(slot, carry):
        pl.semaphore_signal(barrier, inc=1, device_id=partner(slot, 1), device_id_type=MESH)
        return carry

    lax.fori_loop(1, 64, body, 0)
    for device in more:
        pl.semaphore_signal(barrier, inc=1, device_id=device, device_id_type=MESH)
    pl.semaphore_wait(barrier, 63 + len(more))


def experts_kernel(
    outgoing, gain, w_gate, w_up, w_down, back,
    send, recv, sems, sent, came, sent_back, came_back, rows, hidden, results, wide, down, normed,
):
    me = lax.axis_index("head")
    width = outgoing.shape[1]
    cap = outgoing.shape[0] // 64
    inner = w_gate.shape[1]
    many = 8 * cap
    columns = pl.ds(pl.multiple_of(me * width, 128), width)
    own_hidden = pl.ds(pl.multiple_of(me * inner, 128), inner)

    def block(slot):
        return pl.ds(pl.multiple_of(slot * cap, cap), cap)

    def there(slot):
        return pltpu.make_async_remote_copy(
            src_ref=outgoing.at[block(slot), :], dst_ref=rows.at[block(slot), columns],
            send_sem=sent.at[slot], recv_sem=came.at[slot],
            device_id=partner(slot, 1), device_id_type=MESH,
        )

    def home(slot):
        return pltpu.make_async_remote_copy(
            src_ref=results.at[block(slot), :], dst_ref=back.at[block(slot), :],
            send_sem=sent_back.at[slot], recv_sem=came_back.at[slot],
            device_id=partner(slot, -1), device_id_type=MESH,
        )

    def each(first, last, act):
        def body(slot, carry):
            act(slot)
            return carry

        lax.fori_loop(first, last, body, 0)

    def of_chunk(chunk, act):
        each(max(8 * chunk, 1), 8 * chunk + 8, act)

    weights = [
        pltpu.make_async_copy(w_gate, wide.at[:, pl.ds(0, inner)], sems.at[0]),
        pltpu.make_async_copy(w_up, wide.at[:, pl.ds(inner, inner)], sems.at[1]),
        pltpu.make_async_copy(w_down, down, sems.at[2]),
    ]
    own = pltpu.make_async_copy(outgoing.at[block(0), :], rows.at[block(0), columns], sems.at[3])
    own.start()
    for copy in weights:
        copy.start()
    greet_all([near("x", 1), near("x", -1)])
    for chunk in CHUNK_ORDER:
        of_chunk(chunk, lambda slot: there(slot).start())
    own.wait()
    for copy in weights:
        copy.wait()
    copies = Copies(send, recv)
    last = pltpu.make_async_copy(results.at[block(0), :], back.at[block(0), :], sems.at[3])

    def arrive(chunk):
        of_chunk(chunk, lambda slot: there(slot).wait_recv())
        ring_start(copies, ("m", chunk), rows, width, many, many * chunk)

    def pass_rows(chunk):
        ring_relay(copies, ("m", chunk), rows, width, many, many * chunk)

    def gate_up(chunk):
        copies.arrived((("m", chunk), "rr"))
        copies.arrived((("m", chunk), "ll"))
        at = pl.ds(many * chunk, many)
        squares = jnp.zeros((many, 1), jnp.float32)
        for part in range(X):
            piece = rows[at, pl.ds(part * width, width)].astype(jnp.float32)
            squares = squares + jnp.sum(piece * piece, axis=1, keepdims=True)
        factor = lax.rsqrt(squares / (X * width) + NORM_EPS)
        for part in range(X):
            where = pl.ds(part * width, width)
            piece = rows[at, where].astype(jnp.float32)
            normed[:, where] = (piece * factor * gain[:, where].astype(jnp.float32)).astype(normed.dtype)
        both = jnp.dot(normed[...], wide[...], preferred_element_type=jnp.float32)
        gate = both[:, :inner]
        hidden[at, own_hidden] = (gate / (1.0 + jnp.exp(-gate)) * both[:, inner:]).astype(hidden.dtype)

    def send_hidden(chunk):
        of_chunk(chunk, lambda slot: there(slot).wait_send())
        ring_start(copies, ("h", chunk), hidden, inner, many, many * chunk)

    def pass_hidden(chunk):
        ring_relay(copies, ("h", chunk), hidden, inner, many, many * chunk)

    def finish(chunk):
        copies.arrived((("h", chunk), "rr"))
        copies.arrived((("h", chunk), "ll"))
        at = pl.ds(many * chunk, many)
        results[at, :] = jnp.dot(
            hidden[at, :], down[...], preferred_element_type=jnp.float32
        ).astype(results.dtype)

    def send_home(chunk):
        if chunk == 0:
            last.start()
        of_chunk(chunk, lambda slot: home(slot).start())

    stages = ((arrive, 0), (pass_rows, 1), (gate_up, 2), (pass_hidden, 3), (send_hidden, 2), (send_home, 5), (finish, 4))
    for step in range(len(CHUNK_ORDER) + 5):
        for stage, lag in stages:
            if 0 <= step - lag < len(CHUNK_ORDER):
                stage(CHUNK_ORDER[step - lag])
    copies.finish()
    last.wait()
    each(1, 64, lambda slot: home(slot).wait())


def rms_norm(values_in, gain_vector):
    widened = values_in.astype(jnp.float32)
    mean_sq = jnp.mean(widened * widened, axis=-1, keepdims=True)
    return (widened * lax.rsqrt(mean_sq + NORM_EPS) * gain_vector.astype(jnp.float32)).astype(
        jnp.bfloat16
    )


def rotary_tables(token_positions, head_dim):
    half_dim = head_dim // 2
    frequency = jnp.exp(
        jnp.arange(half_dim, dtype=jnp.float32) * (-2.0 * math.log(ROPE_BASE) / head_dim)
    )
    angles = token_positions.astype(jnp.float32)[:, None] * frequency[None, :]
    return jnp.cos(angles), jnp.sin(angles)


def apply_rotary(product, cosine, sine_part):
    half_dim = product.shape[-1] // 2
    first_half = product[..., :half_dim]
    second_half = product[..., half_dim:]
    turned = jnp.concatenate(
        [
            first_half * cosine - second_half * sine_part,
            second_half * cosine + first_half * sine_part,
        ],
        axis=-1,
    )
    return turned.astype(jnp.bfloat16)


def attention_kernel(own, q, kv, own_start, token_index, first, out, send, recv, sems, sk):
    rows, dim = q.shape
    queries = q[...]
    scale = dim ** (-0.5)
    copies_of_mask = rows // own_start.shape[0]

    def step(state, keys, values, bias):
        top, total, summed = state
        scores = lax.dot_general(
            queries, keys, (((1,), (1,)), ((), ())), preferred_element_type=jnp.float32
        ) * scale
        if bias is not None:
            scores = scores + bias
        new_top = jnp.maximum(top, jnp.max(scores, axis=1, keepdims=True))
        weights = jnp.exp(scores - new_top)
        factor = jnp.exp(top - new_top)
        total = total * factor + jnp.sum(weights, axis=1, keepdims=True)
        summed = summed * factor + jnp.dot(
            weights.astype(jnp.bfloat16), values, preferred_element_type=jnp.float32
        )
        return new_top, total, summed

    def prefix(index, state):
        return step(state, kv[index, :, 0].reshape(-1, dim), kv[index, :, 1].reshape(-1, dim), None)

    def suffix(index, state):
        at = first[index, :][None, :]
        visible = (at >= own_start[...]) & (at <= token_index[...])
        bias = jnp.concatenate([jnp.where(visible, 0.0, MASKED)] * copies_of_mask, axis=0)
        return step(state, sk[index, :, 0].reshape(-1, dim), sk[index, :, 1].reshape(-1, dim), bias)

    local([(own, sk.at[0, 0])], sems)
    greet([near("y", 1), near("y", -1), near("z", 1), near("z", -1)])
    up, down, ahead = near("y", 1), near("y", -1), near("z", 1)
    copies = Copies(send, recv)
    torus_start(copies, sk, BACK, 0)
    state = (
        jnp.full((rows, 1), MASKED, jnp.float32),
        jnp.zeros((rows, 1), jnp.float32),
        jnp.zeros((rows, dim), jnp.float32),
    )
    state = lax.fori_loop(0, Y // 2, prefix, state)
    for slot in range(1, BACK + 1):
        copies.arrived(("f", slot))
        if slot < BACK:
            copies.start(("f", slot + 1), sk.at[0, slot], sk.at[0, slot + 1], ahead)
        copies.start(("u", slot), sk.at[0, slot], sk.at[1, slot], up)
        copies.start(("d", slot), sk.at[0, slot], sk.at[3, slot], down)
        if slot == 1:
            copies.arrived(("u", 0))
            copies.start(("v", 0), sk.at[1, 0], sk.at[2, 0], up)
            state = lax.fori_loop(Y // 2, Y, prefix, state)
    state = suffix(0, state)
    copies.arrived(("u", 1))
    copies.start(("v", 1), sk.at[1, 1], sk.at[2, 1], up)
    copies.arrived(("d", 2))
    copies.start(("v", 2), sk.at[3, 2], sk.at[2, 2], down)
    copies.arrived(("u", 2))
    state = suffix(1, state)
    for slot in (0, 1):
        copies.arrived(("d", slot))
    state = suffix(3, state)
    for slot in (0, 1, 2):
        copies.arrived(("v", slot))
    state = suffix(2, state)
    out[...] = (state[2] / state[1]).astype(out.dtype)
    copies.finish()


def on_device(
    hidden_in,
    attn_gain,
    w_query,
    key_projection_weight,
    value_projection_weight,
    w_out,
    prefix_keys,
    cached_prefix_values,
    request_lengths,
    moe_gain,
    expert_ids,
    route_weights,
    w_gate,
    w_up,
    w_down,
):
    f32, bf16 = jnp.float32, jnp.bfloat16
    tok_count = lax.axis_size("tok")
    tok_rank = lax.axis_index("tok")
    head_rank = lax.axis_index("head")
    grp_rank = lax.axis_index("grp")
    tok_dev = hidden_in.shape[1]
    model_width = attn_gain.shape[0]
    head_dim = prefix_keys.shape[3]
    prefix_dev = prefix_keys.shape[1]
    group_length = w_query.shape[1] // head_dim
    share = model_width // X
    quarter = hidden_in[0]

    features, prefix_kv, other_query, other_key, other_value, other_out = call(
        prologue_kernel, 0,
        (quarter, prefix_keys[0, :, 0], cached_prefix_values[0, :, 0], w_query,
         key_projection_weight, value_projection_weight, w_out),
        (shape(tok_dev, model_width), shape(Y, Z, 2, prefix_dev, head_dim), shape(*w_query.shape),
         shape(*key_projection_weight.shape), shape(*value_projection_weight.shape), shape(*w_out.shape)),
        [VM] * 3 + [HB] * 4, [VM] * 2 + [HB] * 4, torus_copies(4, 3) + 8,
    )
    attention_input = rms_norm(features, attn_gain)
    lengths = request_lengths[0]
    request_ends = jnp.cumsum(lengths)
    starts = request_ends - lengths
    token_index = tok_rank * tok_dev + jnp.arange(tok_dev, dtype=jnp.int32)
    own_start = jnp.max(
        jnp.where(starts[None, :] <= token_index[:, None], starts[None, :], 0), axis=1
    )
    token_positions = prefix_dev * tok_count + token_index - own_start
    cosine, sine_part = rotary_tables(token_positions, head_dim)

    half = model_width // 2
    lower = attention_input[:, :half]
    upper = attention_input[:, half:]
    mine = jnp.where(grp_rank == 0, lower, upper)
    others = jnp.where(grp_rank == 0, upper, lower)

    def project(own, other):
        return jnp.dot(mine, own, preferred_element_type=f32) + jnp.dot(
            others, other, preferred_element_type=f32
        )

    query_product = project(w_query, other_query).reshape(tok_dev, group_length, head_dim)
    key_product = project(key_projection_weight, other_key)
    value_product = project(value_projection_weight, other_value)
    queries = apply_rotary(
        jnp.transpose(query_product, (1, 0, 2)), cosine[None], sine_part[None]
    ).reshape(group_length * tok_dev, head_dim)
    suffix_own = jnp.stack(
        [apply_rotary(key_product, cosine, sine_part), value_product.astype(bf16)]
    )
    z_rank, y_rank = tok_rank // Y, tok_rank % Y
    y_from = (y_rank - jnp.arange(Y) + Y) % Y
    z_from = z_rank - jnp.arange(BACK + 1)
    device_from = jnp.where(z_from[None, :] >= 0, z_from[None, :] * Y + y_from[:, None], tok_count)
    key_index = (
        device_from[:, :, None] * tok_dev + jnp.arange(tok_dev, dtype=jnp.int32)
    ).reshape(Y, (BACK + 1) * tok_dev)
    rows = group_length * tok_dev
    attended = call(
        attention_kernel, 1,
        (suffix_own, queries, prefix_kv, own_start[:, None], token_index[:, None],
         key_index.astype(jnp.int32)),
        shape(rows, head_dim), [VM] * 6, VM, torus_copies(BACK, 0),
        (pltpu.VMEM((Y, BACK + 1, 2, tok_dev, head_dim), bf16),),
    )
    attended = jnp.transpose(attended.reshape(group_length, tok_dev, head_dim), (1, 0, 2)).reshape(
        tok_dev, group_length * head_dim
    )

    def out_part(weights):
        return lax.dot_general(
            attended, weights, (((1,), (1,)), ((), ())), preferred_element_type=f32
        ).astype(bf16)

    own_part, other_part = out_part(w_out), out_part(other_out)
    first_part = jnp.where(grp_rank == 0, own_part, other_part)
    second_part = jnp.where(grp_rank == 0, other_part, own_part)
    parts = jnp.stack(
        [first_part[:, :share], first_part[:, share:], second_part[:, :share], second_part[:, share:]]
    )
    got = call(
        exchange_kernel, 2, (parts,), shape(X - 1, tok_dev, share), [VM], VM, 6,
        (pltpu.VMEM((2, tok_dev // 2, share), bf16),),
    )
    own_share = lax.dynamic_index_in_dim(parts, head_rank, 0, keepdims=False)
    mid = (
        quarter.astype(f32)
        + (own_share.astype(f32) + got[0].astype(f32) + got[1].astype(f32) + got[2].astype(f32))
    ).astype(bf16)
    mid_wide = mid.astype(f32)
    experts = 2 * tok_count * w_gate.shape[0]
    top_count = expert_ids.shape[2]
    capacity = 4 * tok_dev * top_count // (3 * experts)
    chosen = expert_ids[0]
    e_grp, e_tok = chosen // tok_count, chosen % tok_count
    relative = (
        ((e_tok // Y - z_rank + Z) % Z) * 8
        + ((e_tok % Y - y_rank + Y) % Y) * 2
        + (e_grp + grp_rank) % 2
    )
    hit = relative[:, :, None] == jnp.arange(experts, dtype=jnp.int32)[None, None, :]
    uses = jnp.any(hit, axis=1)
    weight = jnp.sum(jnp.where(hit, route_weights[0][:, :, None], 0.0), axis=1)
    weight_hi = weight.astype(bf16)
    weight_lo = (weight - weight_hi.astype(f32)).astype(bf16)
    earlier = jnp.tril(jnp.ones((tok_dev, tok_dev), bf16), -1)
    rank = jnp.dot(earlier, uses.astype(bf16), preferred_element_type=f32)
    rank = jnp.where(uses, rank, -1.0).astype(bf16)
    slots = experts * capacity
    slot_index = jnp.arange(slots, dtype=jnp.int32)
    spread = (slot_index[None, :] // capacity == jnp.arange(experts, dtype=jnp.int32)[:, None]).astype(bf16)
    spread_rank = jnp.dot(rank, spread, preferred_element_type=f32)
    placed = spread_rank == (slot_index % capacity).astype(f32)[None, :]
    outgoing = lax.dot_general(
        placed.astype(bf16), mid, (((0,), (0,)), ((), ())), preferred_element_type=f32
    ).astype(bf16)

    inner = w_gate.shape[2]
    returned = call(
        experts_kernel, 4, (outgoing, moe_gain[None, :], w_gate[0], w_up[0], w_down[0]), shape(slots, share),
        [VM] * 2 + [HB] * 3, VM, 2 * 8 * 4,
        (
            *[pltpu.SemaphoreType.DMA((64,))] * 4,
            pltpu.VMEM((slots, model_width), bf16),
            pltpu.VMEM((slots, X * inner), bf16),
            pltpu.VMEM((slots, share), bf16),
            pltpu.VMEM((model_width, 2 * inner), bf16),
            pltpu.VMEM((X * inner, share), bf16),
            pltpu.VMEM((8 * capacity, model_width), bf16),
        ),
    )

    def combine(part):
        spread_weight = jnp.where(placed, jnp.dot(part, spread, preferred_element_type=f32), 0.0)
        return jnp.dot(spread_weight.astype(bf16), returned, preferred_element_type=f32)

    output = (mid_wide + (combine(weight_hi) + combine(weight_lo))).astype(bf16)
    return output[None]


def solution(mesh):
    return jax.shard_map(
        on_device,
        mesh=mesh,
        in_specs=(
            P("grp", "tok", "head"),
            P(),
            P("grp", "head"),
            P("grp", "head"),
            P("grp", "head"),
            P("grp", "head"),
            P("grp", "tok", "head", None),
            P("grp", "tok", "head", None),
            P("grp", None),
            P(),
            P("grp", "tok", None),
            P("grp", "tok", None),
            P(("grp", "tok"), None, "head"),
            P(("grp", "tok"), None, "head"),
            P(("grp", "tok"), None, "head"),
        ),
        out_specs=P("grp", "tok", "head"),
        check_vma=False,
    )
```

```python
import functools
import math

import jax
import jax.numpy as jnp
from jax import lax
from jax.experimental import pallas as pl
from jax.experimental.pallas import tpu as pltpu
from jax.sharding import PartitionSpec as P

ROPE_BASE = 500000.0
NORM_EPS = 1e-06
MASKED = -1e30
MESH = pl.DeviceIdType.MESH
Z, Y, X = 8, 4, 4
CHUNK_ORDER = (0, 1, 5, 3, 4, 6, 2, 7)
BACK = 2


class Copies:
    def __init__(self, send, recv):
        self.send, self.recv, self.made, self.open = send, recv, {}, []

    def start(self, key, src, dst, device):
        at = len(self.made)
        copy = pltpu.make_async_remote_copy(
            src_ref=src, dst_ref=dst, send_sem=self.send.at[at], recv_sem=self.recv.at[at],
            device_id=device, device_id_type=MESH,
        )
        copy.start()
        self.made[key] = copy
        self.open.append(key)

    def arrived(self, key):
        self.made[key].wait_recv()
        self.open.remove(key)

    def finish(self):
        for key in list(self.open):
            self.arrived(key)
        for copy in self.made.values():
            copy.wait_send()


def near(axis, step):
    if axis == "x":
        return {"head": lax.rem(lax.axis_index("head") + (step + X), X)}
    if axis == "core":
        return {"grp": 1 - lax.axis_index("grp")}
    tok = lax.axis_index("tok")
    z, y = tok // Y, lax.rem(tok, Y)
    if axis == "z":
        z = lax.rem(z + (step + Z), Z)
    else:
        y = lax.rem(y + (step + Y), Y)
    return {"tok": z * Y + y}


def greet(devices):
    barrier = pltpu.get_barrier_semaphore()
    for device in devices:
        pl.semaphore_signal(barrier, inc=1, device_id=device, device_id_type=MESH)
    pl.semaphore_wait(barrier, len(devices))


def torus_start(copies, kv, forward, backward):
    up, down = near("y", 1), near("y", -1)
    if forward:
        copies.start(("f", 1), kv.at[0, 0], kv.at[0, 1], near("z", 1))
    if backward:
        copies.start(("b", 1), kv.at[0, 0], kv.at[0, forward + backward], near("z", -1))
    copies.start(("u", 0), kv.at[0, 0], kv.at[1, 0], up)
    copies.start(("d", 0), kv.at[0, 0], kv.at[3, 0], down)


def torus_step(copies, kv, forward, backward, step):
    up, down = near("y", 1), near("y", -1)
    last = forward + backward
    for mark, reach, slot, following, way in (
        ("f", forward, step, step + 1, 1),
        ("b", backward, last + 1 - step, last - step, -1),
    ):
        if step > reach:
            continue
        copies.arrived((mark, step))
        if step < reach:
            copies.start((mark, step + 1), kv.at[0, slot], kv.at[0, following], near("z", way))
        copies.start(("u", slot), kv.at[0, slot], kv.at[1, slot], up)
        copies.start(("d", slot), kv.at[0, slot], kv.at[3, slot], down)


def torus_cross(copies, kv, last, *slots):
    for slot in slots:
        if slot <= (last + 1) // 2:
            copies.arrived(("u", slot))
            copies.start(("v", slot), kv.at[1, slot], kv.at[2, slot], near("y", 1))
        else:
            copies.arrived(("d", slot))
            copies.start(("v", slot), kv.at[3, slot], kv.at[2, slot], near("y", -1))


def column(copies, mark):
    for key in [key for key in copies.open if key[0] == mark]:
        copies.arrived(key)


def torus_copies(forward, backward):
    slots = forward + backward + 1
    return forward + backward + 3 * slots


def ring_start(copies, key, ref, width, rows, offset):
    me = lax.axis_index("head")
    own = ref.at[pl.ds(offset, rows), pl.ds(pl.multiple_of(me * width, 128), width)]
    copies.start((key, "r"), own, own, near("x", 1))
    copies.start((key, "l"), own, own, near("x", -1))


def ring_relay(copies, key, ref, width, rows, offset):
    me = lax.axis_index("head")
    half = rows // 2
    copies.arrived((key, "r"))
    left = lax.rem(me + (X - 1), X)
    first = ref.at[pl.ds(offset, half), pl.ds(pl.multiple_of(left * width, 128), width)]
    copies.start((key, "rr"), first, first, near("x", 1))
    copies.arrived((key, "l"))
    right = lax.rem(me + 1, X)
    second = ref.at[pl.ds(offset + half, half), pl.ds(pl.multiple_of(right * width, 128), width)]
    copies.start((key, "ll"), second, second, near("x", -1))


def local(pairs, sems):
    made = [pltpu.make_async_copy(a, b, sems.at[i]) for i, (a, b) in enumerate(pairs)]
    for copy in made:
        copy.start()
    for copy in made:
        copy.wait()


VM = pl.BlockSpec(memory_space=pltpu.VMEM)
HB = pl.BlockSpec(memory_space=pl.ANY)


def call(kernel, ident, ins, outs, in_specs, out_specs, copies, extra=()):
    return pl.pallas_call(
        kernel,
        out_shape=outs,
        in_specs=in_specs,
        out_specs=out_specs,
        scratch_shapes=[
            pltpu.SemaphoreType.DMA((copies,)),
            pltpu.SemaphoreType.DMA((copies,)),
            pltpu.SemaphoreType.DMA((6,)),
            *extra,
        ],
        compiler_params=pltpu.CompilerParams(collective_id=ident, has_side_effects=True),
    )(*ins)


def shape(*dims, dtype=jnp.bfloat16):
    return jax.ShapeDtypeStruct(dims, dtype)


def front_kernel(
    hid, gain, pk, pv, wq, wk, wv, wo, cosine, sine, own_start, token_index, first, out, wo2,
    send, recv, sems, send2, recv2, feat, normed, kv, sk, wide, queries,
):
    me, grp = lax.axis_index("head"), lax.axis_index("grp")
    tokens, width = hid.shape
    depth, across = wq.shape
    dim = pk.shape[1]
    heads = across // dim
    rows = heads * tokens
    scale = dim ** (-0.5)
    mine = pl.ds(pl.multiple_of(grp * depth, depth), depth)
    places = [
        (wq, wide.at[mine, pl.ds(0, across)]),
        (wk, wide.at[mine, pl.ds(across, dim)]),
        (wv, wide.at[mine, pl.ds(across + dim, dim)]),
    ]
    own_weights = [pltpu.make_async_copy(a, b, sems.at[3 + i]) for i, (a, b) in enumerate(places)]
    for copy in own_weights:
        copy.start()
    local(
        [
            (pk, kv.at[0, 0, 0]),
            (pv, kv.at[0, 0, 1]),
            (hid, feat.at[:, pl.ds(pl.multiple_of(me * width, 128), width)]),
        ],
        sems,
    )
    core = near("core", 1)
    greet([near("x", 1), near("x", -1), near("y", 1), near("y", -1), near("z", 1), near("z", -1), core])
    copies = Copies(send, recv)
    torus_start(copies, kv, 4, 3)
    ring_start(copies, "h", feat, width, tokens, 0)
    for key, (a, b) in zip(("wq", "wk", "wv"), places):
        copies.start(key, a, b, core)
    copies.start("wo", wo, wo2, core)
    torus_step(copies, kv, 4, 3, 1)
    ring_relay(copies, "h", feat, width, tokens, 0)
    torus_step(copies, kv, 4, 3, 2)
    torus_cross(copies, kv, 7, 0, 1, 7)
    torus_step(copies, kv, 4, 3, 3)

    copies.arrived(("h", "rr"))
    copies.arrived(("h", "ll"))
    for copy in own_weights:
        copy.wait()
    for key in ("wq", "wk", "wv"):
        copies.arrived(key)
    squares = jnp.zeros((tokens, 1), jnp.float32)
    for part in range(X):
        piece = feat[:, pl.ds(part * width, width)].astype(jnp.float32)
        squares = squares + jnp.sum(piece * piece, axis=1, keepdims=True)
    factor = lax.rsqrt(squares / (X * width) + NORM_EPS)
    for part in range(X):
        where = pl.ds(part * width, width)
        piece = feat[:, where].astype(jnp.float32)
        normed[:, where] = (piece * factor * gain[:, where].astype(jnp.float32)).astype(normed.dtype)
    product = jnp.dot(normed[...], wide[...], preferred_element_type=jnp.float32)

    def turned(head):
        part = product[:, head * dim : (head + 1) * dim]
        return (part * cosine[...] + pltpu.roll(part, dim // 2, 1) * sine[...]).astype(jnp.bfloat16)

    sk[0, 0, 0] = turned(heads)
    sk[0, 0, 1] = product[:, across + dim :].astype(jnp.bfloat16)
    for head in range(heads):
        queries[pl.ds(head * tokens, tokens), :] = turned(head)

    torus_step(copies, kv, 4, 3, 4)
    torus_cross(copies, kv, 7, 2, 6)
    later = Copies(send2, recv2)
    torus_start(later, sk, BACK, 0)

    def step(state, keys, values, bias):
        top, total, summed = state
        scores = lax.dot_general(
            queries[...], keys, (((1,), (1,)), ((), ())), preferred_element_type=jnp.float32
        ) * scale
        if bias is not None:
            scores = scores + bias
        new_top = jnp.maximum(top, jnp.max(scores, axis=1, keepdims=True))
        weights = jnp.exp(scores - new_top)
        shrink = jnp.exp(top - new_top)
        total = total * shrink + jnp.sum(weights, axis=1, keepdims=True)
        summed = summed * shrink + jnp.dot(
            weights.astype(jnp.bfloat16), values, preferred_element_type=jnp.float32
        )
        return new_top, total, summed

    def prefix(index, state):
        return step(state, kv[index, :, 0].reshape(-1, dim), kv[index, :, 1].reshape(-1, dim), None)

    def suffix(index, state):
        at = first[index, :][None, :]
        visible = (at >= own_start[...]) & (at <= token_index[...])
        bias = jnp.concatenate([jnp.where(visible, 0.0, MASKED)] * heads, axis=0)
        return step(state, sk[index, :, 0].reshape(-1, dim), sk[index, :, 1].reshape(-1, dim), bias)

    state = (
        jnp.full((rows, 1), MASKED, jnp.float32),
        jnp.zeros((rows, 1), jnp.float32),
        jnp.zeros((rows, dim), jnp.float32),
    )
    state = prefix(0, state)
    torus_cross(copies, kv, 7, 3, 5, 4)
    torus_step(later, sk, BACK, 0, 1)
    column(copies, "u")
    state = prefix(1, state)
    torus_step(later, sk, BACK, 0, 2)
    torus_cross(later, sk, BACK, 0)
    column(copies, "d")
    state = prefix(3, state)
    torus_cross(later, sk, BACK, 1, 2)
    column(copies, "v")
    state = prefix(2, state)
    state = suffix(0, state)
    column(later, "u")
    state = suffix(1, state)
    column(later, "d")
    state = suffix(3, state)
    column(later, "v")
    _, total, summed = suffix(2, state)
    result = summed / total
    for head in range(heads):
        out[:, head * dim : (head + 1) * dim] = result[head * tokens : (head + 1) * tokens].astype(out.dtype)
    copies.finish()
    later.finish()


def exchange_kernel(parts, got, send, recv, sems, transit):
    me = lax.axis_index("head")
    half = parts.shape[1] // 2
    greet([near("x", 1), near("x", -1)])
    copies = Copies(send, recv)
    right, left, opposite = (lax.rem(me + d, X) for d in (1, 3, 2))
    copies.start("tr", parts.at[opposite, pl.ds(0, half)], transit.at[0], near("x", 1))
    copies.start("tl", parts.at[opposite, pl.ds(half, half)], transit.at[1], near("x", -1))
    copies.start("r", parts.at[right], got.at[0], near("x", 1))
    copies.start("l", parts.at[left], got.at[2], near("x", -1))
    copies.arrived("tr")
    copies.start("rr", transit.at[0], got.at[1, pl.ds(0, half)], near("x", 1))
    copies.arrived("tl")
    copies.start("ll", transit.at[1], got.at[1, pl.ds(half, half)], near("x", -1))
    copies.finish()


def partner(slot, sign):
    tok = lax.axis_index("tok")
    grp = lax.axis_index("grp")
    dz, dy, dg = slot // 8, lax.rem(slot // 2, 4), lax.rem(slot, 2)
    z = lax.rem(tok // Y + Z + sign * dz, Z)
    y = lax.rem(lax.rem(tok, Y) + Y + sign * dy, Y)
    return {"grp": lax.rem(grp + dg, 2), "tok": z * Y + y}


def greet_all(more):
    barrier = pltpu.get_barrier_semaphore()

    def body(slot, carry):
        pl.semaphore_signal(barrier, inc=1, device_id=partner(slot, 1), device_id_type=MESH)
        return carry

    lax.fori_loop(1, 64, body, 0)
    for device in more:
        pl.semaphore_signal(barrier, inc=1, device_id=device, device_id_type=MESH)
    pl.semaphore_wait(barrier, 63 + len(more))


def experts_kernel(
    outgoing, gain, w_gate, w_up, w_down, back,
    send, recv, sems, sent, came, sent_back, came_back, rows, hidden, results, wide, down, normed,
):
    me = lax.axis_index("head")
    width = outgoing.shape[1]
    cap = outgoing.shape[0] // 64
    inner = w_gate.shape[1]
    many = 8 * cap
    columns = pl.ds(pl.multiple_of(me * width, 128), width)
    own_hidden = pl.ds(pl.multiple_of(me * inner, 128), inner)

    def block(slot):
        return pl.ds(pl.multiple_of(slot * cap, cap), cap)

    def there(slot):
        return pltpu.make_async_remote_copy(
            src_ref=outgoing.at[block(slot), :], dst_ref=rows.at[block(slot), columns],
            send_sem=sent.at[slot], recv_sem=came.at[slot],
            device_id=partner(slot, 1), device_id_type=MESH,
        )

    def home(slot):
        return pltpu.make_async_remote_copy(
            src_ref=results.at[block(slot), :], dst_ref=back.at[block(slot), :],
            send_sem=sent_back.at[slot], recv_sem=came_back.at[slot],
            device_id=partner(slot, -1), device_id_type=MESH,
        )

    def each(first, last, act):
        def body(slot, carry):
            act(slot)
            return carry

        lax.fori_loop(first, last, body, 0)

    def of_chunk(chunk, act):
        each(max(8 * chunk, 1), 8 * chunk + 8, act)

    weights = [
        pltpu.make_async_copy(w_gate, wide.at[:, pl.ds(0, inner)], sems.at[0]),
        pltpu.make_async_copy(w_up, wide.at[:, pl.ds(inner, inner)], sems.at[1]),
        pltpu.make_async_copy(w_down, down, sems.at[2]),
    ]
    own = pltpu.make_async_copy(outgoing.at[block(0), :], rows.at[block(0), columns], sems.at[3])
    own.start()
    for copy in weights:
        copy.start()
    greet_all([near("x", 1), near("x", -1)])
    for chunk in CHUNK_ORDER:
        of_chunk(chunk, lambda slot: there(slot).start())
    own.wait()
    for copy in weights:
        copy.wait()
    copies = Copies(send, recv)
    last = pltpu.make_async_copy(results.at[block(0), :], back.at[block(0), :], sems.at[3])

    def arrive(chunk):
        of_chunk(chunk, lambda slot: there(slot).wait_recv())
        ring_start(copies, ("m", chunk), rows, width, many, many * chunk)

    def pass_rows(chunk):
        ring_relay(copies, ("m", chunk), rows, width, many, many * chunk)

    def gate_up(chunk):
        copies.arrived((("m", chunk), "rr"))
        copies.arrived((("m", chunk), "ll"))
        at = pl.ds(many * chunk, many)
        squares = jnp.zeros((many, 1), jnp.float32)
        for part in range(X):
            piece = rows[at, pl.ds(part * width, width)].astype(jnp.float32)
            squares = squares + jnp.sum(piece * piece, axis=1, keepdims=True)
        factor = lax.rsqrt(squares / (X * width) + NORM_EPS)
        for part in range(X):
            where = pl.ds(part * width, width)
            piece = rows[at, where].astype(jnp.float32)
            normed[:, where] = (piece * factor * gain[:, where].astype(jnp.float32)).astype(normed.dtype)
        both = jnp.dot(normed[...], wide[...], preferred_element_type=jnp.float32)
        gate = both[:, :inner]
        hidden[at, own_hidden] = (gate / (1.0 + jnp.exp(-gate)) * both[:, inner:]).astype(hidden.dtype)

    def send_hidden(chunk):
        of_chunk(chunk, lambda slot: there(slot).wait_send())
        ring_start(copies, ("h", chunk), hidden, inner, many, many * chunk)

    def pass_hidden(chunk):
        ring_relay(copies, ("h", chunk), hidden, inner, many, many * chunk)

    def finish(chunk):
        copies.arrived((("h", chunk), "rr"))
        copies.arrived((("h", chunk), "ll"))
        at = pl.ds(many * chunk, many)
        results[at, :] = jnp.dot(
            hidden[at, :], down[...], preferred_element_type=jnp.float32
        ).astype(results.dtype)

    def send_home(chunk):
        if chunk == 0:
            last.start()
        of_chunk(chunk, lambda slot: home(slot).start())

    stages = ((arrive, 0), (pass_rows, 1), (gate_up, 2), (pass_hidden, 3), (send_hidden, 2), (send_home, 5), (finish, 4))
    for step in range(len(CHUNK_ORDER) + 5):
        for stage, lag in stages:
            if 0 <= step - lag < len(CHUNK_ORDER):
                stage(CHUNK_ORDER[step - lag])
    copies.finish()
    last.wait()
    each(1, 64, lambda slot: home(slot).wait())


def rotary_tables(token_positions, head_dim):
    half_dim = head_dim // 2
    frequency = jnp.exp(
        jnp.arange(half_dim, dtype=jnp.float32) * (-2.0 * math.log(ROPE_BASE) / head_dim)
    )
    angles = token_positions.astype(jnp.float32)[:, None] * frequency[None, :]
    return jnp.cos(angles), jnp.sin(angles)


def on_device(
    hidden_in,
    attn_gain,
    w_query,
    key_projection_weight,
    value_projection_weight,
    w_out,
    prefix_keys,
    cached_prefix_values,
    request_lengths,
    moe_gain,
    expert_ids,
    route_weights,
    w_gate,
    w_up,
    w_down,
):
    f32, bf16 = jnp.float32, jnp.bfloat16
    tok_count = lax.axis_size("tok")
    tok_rank = lax.axis_index("tok")
    head_rank = lax.axis_index("head")
    grp_rank = lax.axis_index("grp")
    tok_dev = hidden_in.shape[1]
    model_width = attn_gain.shape[0]
    head_dim = prefix_keys.shape[3]
    prefix_dev = prefix_keys.shape[1]
    group_length = w_query.shape[1] // head_dim
    share = model_width // X
    quarter = hidden_in[0]

    lengths = request_lengths[0]
    request_ends = jnp.cumsum(lengths)
    starts = request_ends - lengths
    token_index = tok_rank * tok_dev + jnp.arange(tok_dev, dtype=jnp.int32)
    own_start = jnp.max(
        jnp.where(starts[None, :] <= token_index[:, None], starts[None, :], 0), axis=1
    )
    token_positions = prefix_dev * tok_count + token_index - own_start
    cosine, sine_part = rotary_tables(token_positions, head_dim)

    z_rank, y_rank = tok_rank // Y, tok_rank % Y
    y_from = (y_rank - jnp.arange(Y) + Y) % Y
    z_from = z_rank - jnp.arange(BACK + 1)
    device_from = jnp.where(z_from[None, :] >= 0, z_from[None, :] * Y + y_from[:, None], tok_count)
    key_index = (
        device_from[:, :, None] * tok_dev + jnp.arange(tok_dev, dtype=jnp.int32)
    ).reshape(Y, (BACK + 1) * tok_dev)
    attended, other_out = call(
        front_kernel, 0,
        (quarter, attn_gain[None, :], prefix_keys[0, :, 0], cached_prefix_values[0, :, 0], w_query,
         key_projection_weight, value_projection_weight, w_out,
         jnp.concatenate([cosine, cosine], axis=1), jnp.concatenate([-sine_part, sine_part], axis=1),
         own_start[:, None], token_index[:, None], key_index.astype(jnp.int32)),
        (shape(tok_dev, group_length * head_dim), shape(*w_out.shape)),
        [VM] * 4 + [HB] * 4 + [VM] * 5, [VM, HB], torus_copies(4, 3) + 8,
        (
            *[pltpu.SemaphoreType.DMA((torus_copies(BACK, 0),))] * 2,
            pltpu.VMEM((tok_dev, model_width), bf16),
            pltpu.VMEM((tok_dev, model_width), bf16),
            pltpu.VMEM((Y, Z, 2, prefix_dev, head_dim), bf16),
            pltpu.VMEM((Y, BACK + 1, 2, tok_dev, head_dim), bf16),
            pltpu.VMEM((model_width, (group_length + 2) * head_dim), bf16),
            pltpu.VMEM((group_length * tok_dev, head_dim), bf16),
        ),
    )

    def out_part(weights):
        return lax.dot_general(
            attended, weights, (((1,), (1,)), ((), ())), preferred_element_type=f32
        ).astype(bf16)

    own_part, other_part = out_part(w_out), out_part(other_out)
    first_part = jnp.where(grp_rank == 0, own_part, other_part)
    second_part = jnp.where(grp_rank == 0, other_part, own_part)
    parts = jnp.stack(
        [first_part[:, :share], first_part[:, share:], second_part[:, :share], second_part[:, share:]]
    )
    got = call(
        exchange_kernel, 2, (parts,), shape(X - 1, tok_dev, share), [VM], VM, 6,
        (pltpu.VMEM((2, tok_dev // 2, share), bf16),),
    )
    own_share = lax.dynamic_index_in_dim(parts, head_rank, 0, keepdims=False)
    mid = (
        quarter.astype(f32)
        + (own_share.astype(f32) + got[0].astype(f32) + got[1].astype(f32) + got[2].astype(f32))
    ).astype(bf16)
    mid_wide = mid.astype(f32)
    experts = 2 * tok_count * w_gate.shape[0]
    top_count = expert_ids.shape[2]
    capacity = 4 * tok_dev * top_count // (3 * experts)
    chosen = expert_ids[0]
    e_grp, e_tok = chosen // tok_count, chosen % tok_count
    relative = (
        ((e_tok // Y - z_rank + Z) % Z) * 8
        + ((e_tok % Y - y_rank + Y) % Y) * 2
        + (e_grp + grp_rank) % 2
    )
    hit = relative[:, :, None] == jnp.arange(experts, dtype=jnp.int32)[None, None, :]
    uses = jnp.any(hit, axis=1)
    weight = jnp.sum(jnp.where(hit, route_weights[0][:, :, None], 0.0), axis=1)
    weight_hi = weight.astype(bf16)
    weight_lo = (weight - weight_hi.astype(f32)).astype(bf16)
    earlier = jnp.tril(jnp.ones((tok_dev, tok_dev), bf16), -1)
    rank = jnp.dot(earlier, uses.astype(bf16), preferred_element_type=f32)
    rank = jnp.where(uses, rank, -1.0).astype(bf16)
    slots = experts * capacity
    slot_index = jnp.arange(slots, dtype=jnp.int32)
    spread = (slot_index[None, :] // capacity == jnp.arange(experts, dtype=jnp.int32)[:, None]).astype(bf16)
    spread_rank = jnp.dot(rank, spread, preferred_element_type=f32)
    placed = spread_rank == (slot_index % capacity).astype(f32)[None, :]
    outgoing = lax.dot_general(
        placed.astype(bf16), mid, (((0,), (0,)), ((), ())), preferred_element_type=f32
    ).astype(bf16)

    inner = w_gate.shape[2]
    returned = call(
        experts_kernel, 4, (outgoing, moe_gain[None, :], w_gate[0], w_up[0], w_down[0]), shape(slots, share),
        [VM] * 2 + [HB] * 3, VM, 2 * 8 * 4,
        (
            *[pltpu.SemaphoreType.DMA((64,))] * 4,
            pltpu.VMEM((slots, model_width), bf16),
            pltpu.VMEM((slots, X * inner), bf16),
            pltpu.VMEM((slots, share), bf16),
            pltpu.VMEM((model_width, 2 * inner), bf16),
            pltpu.VMEM((X * inner, share), bf16),
            pltpu.VMEM((8 * capacity, model_width), bf16),
        ),
    )

    def combine(part):
        spread_weight = jnp.where(placed, jnp.dot(part, spread, preferred_element_type=f32), 0.0)
        return jnp.dot(spread_weight.astype(bf16), returned, preferred_element_type=f32)

    output = (mid_wide + (combine(weight_hi) + combine(weight_lo))).astype(bf16)
    return output[None]


def solution(mesh):
    return jax.shard_map(
        on_device,
        mesh=mesh,
        in_specs=(
            P("grp", "tok", "head"),
            P(),
            P("grp", "head"),
            P("grp", "head"),
            P("grp", "head"),
            P("grp", "head"),
            P("grp", "tok", "head", None),
            P("grp", "tok", "head", None),
            P("grp", None),
            P(),
            P("grp", "tok", None),
            P("grp", "tok", None),
            P(("grp", "tok"), None, "head"),
            P(("grp", "tok"), None, "head"),
            P(("grp", "tok"), None, "head"),
        ),
        out_specs=P("grp", "tok", "head"),
        check_vma=False,
    )
```

```python
import functools
import math

import jax
import jax.numpy as jnp
from jax import lax
from jax.experimental import pallas as pl
from jax.experimental.pallas import tpu as pltpu
from jax.sharding import PartitionSpec as P

ROPE_BASE = 500000.0
NORM_EPS = 1e-06
MASKED = -1e30
MESH = pl.DeviceIdType.MESH
Z, Y, X = 8, 4, 4
CHUNK_ORDER = (0, 1, 5, 3, 4, 6, 2, 7)
BACK = 2


class Copies:
    def __init__(self, send, recv):
        self.send, self.recv, self.made, self.open = send, recv, {}, []

    def start(self, key, src, dst, device):
        at = len(self.made)
        copy = pltpu.make_async_remote_copy(
            src_ref=src, dst_ref=dst, send_sem=self.send.at[at], recv_sem=self.recv.at[at],
            device_id=device, device_id_type=MESH,
        )
        copy.start()
        self.made[key] = copy
        self.open.append(key)

    def arrived(self, key):
        self.made[key].wait_recv()
        self.open.remove(key)

    def finish(self):
        for key in list(self.open):
            self.arrived(key)
        for copy in self.made.values():
            copy.wait_send()


def near(axis, step):
    if axis == "x":
        return {"head": lax.rem(lax.axis_index("head") + (step + X), X)}
    if axis == "core":
        return {"grp": 1 - lax.axis_index("grp")}
    tok = lax.axis_index("tok")
    z, y = tok // Y, lax.rem(tok, Y)
    if axis == "z":
        z = lax.rem(z + (step + Z), Z)
    else:
        y = lax.rem(y + (step + Y), Y)
    return {"tok": z * Y + y}


def greet(devices):
    barrier = pltpu.get_barrier_semaphore()
    for device in devices:
        pl.semaphore_signal(barrier, inc=1, device_id=device, device_id_type=MESH)
    pl.semaphore_wait(barrier, len(devices))


def torus_start(copies, kv, forward, backward):
    up, down = near("y", 1), near("y", -1)
    if forward:
        copies.start(("f", 1), kv.at[0, 0], kv.at[0, 1], near("z", 1))
    if backward:
        copies.start(("b", 1), kv.at[0, 0], kv.at[0, forward + backward], near("z", -1))
    copies.start(("u", 0), kv.at[0, 0], kv.at[1, 0], up)
    copies.start(("d", 0), kv.at[0, 0], kv.at[3, 0], down)


def torus_step(copies, kv, forward, backward, step):
    up, down = near("y", 1), near("y", -1)
    last = forward + backward
    for mark, reach, slot, following, way in (
        ("f", forward, step, step + 1, 1),
        ("b", backward, last + 1 - step, last - step, -1),
    ):
        if step > reach:
            continue
        copies.arrived((mark, step))
        if step < reach:
            copies.start((mark, step + 1), kv.at[0, slot], kv.at[0, following], near("z", way))
        copies.start(("u", slot), kv.at[0, slot], kv.at[1, slot], up)
        copies.start(("d", slot), kv.at[0, slot], kv.at[3, slot], down)


def torus_cross(copies, kv, last, *slots):
    for slot in slots:
        if slot <= (last + 1) // 2:
            copies.arrived(("u", slot))
            copies.start(("v", slot), kv.at[1, slot], kv.at[2, slot], near("y", 1))
        else:
            copies.arrived(("d", slot))
            copies.start(("v", slot), kv.at[3, slot], kv.at[2, slot], near("y", -1))


def column(copies, mark):
    for key in [key for key in copies.open if key[0] == mark]:
        copies.arrived(key)


def torus_copies(forward, backward):
    slots = forward + backward + 1
    return forward + backward + 3 * slots


def ring_start(copies, key, ref, width, rows, offset):
    me = lax.axis_index("head")
    own = ref.at[pl.ds(offset, rows), pl.ds(pl.multiple_of(me * width, 128), width)]
    copies.start((key, "r"), own, own, near("x", 1))
    copies.start((key, "l"), own, own, near("x", -1))


def ring_relay(copies, key, ref, width, rows, offset):
    me = lax.axis_index("head")
    half = rows // 2
    copies.arrived((key, "r"))
    left = lax.rem(me + (X - 1), X)
    first = ref.at[pl.ds(offset, half), pl.ds(pl.multiple_of(left * width, 128), width)]
    copies.start((key, "rr"), first, first, near("x", 1))
    copies.arrived((key, "l"))
    right = lax.rem(me + 1, X)
    second = ref.at[pl.ds(offset + half, half), pl.ds(pl.multiple_of(right * width, 128), width)]
    copies.start((key, "ll"), second, second, near("x", -1))


def local(pairs, sems):
    made = [pltpu.make_async_copy(a, b, sems.at[i]) for i, (a, b) in enumerate(pairs)]
    for copy in made:
        copy.start()
    for copy in made:
        copy.wait()


VM = pl.BlockSpec(memory_space=pltpu.VMEM)
HB = pl.BlockSpec(memory_space=pl.ANY)


def call(kernel, ident, ins, outs, in_specs, out_specs, copies, extra=()):
    return pl.pallas_call(
        kernel,
        out_shape=outs,
        in_specs=in_specs,
        out_specs=out_specs,
        scratch_shapes=[
            pltpu.SemaphoreType.DMA((copies,)),
            pltpu.SemaphoreType.DMA((copies,)),
            pltpu.SemaphoreType.DMA((6,)),
            *extra,
        ],
        compiler_params=pltpu.CompilerParams(collective_id=ident, has_side_effects=True),
    )(*ins)


def shape(*dims, dtype=jnp.bfloat16):
    return jax.ShapeDtypeStruct(dims, dtype)


def front_kernel(
    hid, gain, pk, pv, wq, wk, wv, wo, cosine, sine, own_start, token_index, first, out, wo2,
    send, recv, sems, send2, recv2, feat, normed, kv, sk, wide, queries,
):
    me, grp = lax.axis_index("head"), lax.axis_index("grp")
    tokens, width = hid.shape
    depth, across = wq.shape
    dim = pk.shape[1]
    heads = across // dim
    rows = heads * tokens
    scale = dim ** (-0.5)
    mine = pl.ds(pl.multiple_of(grp * depth, depth), depth)
    places = [
        (wq, wide.at[mine, pl.ds(0, across)]),
        (wk, wide.at[mine, pl.ds(across, dim)]),
        (wv, wide.at[mine, pl.ds(across + dim, dim)]),
    ]
    own_weights = [pltpu.make_async_copy(a, b, sems.at[3 + i]) for i, (a, b) in enumerate(places)]
    for copy in own_weights:
        copy.start()
    local(
        [
            (pk, kv.at[0, 0, 0]),
            (pv, kv.at[0, 0, 1]),
            (hid, feat.at[:, pl.ds(pl.multiple_of(me * width, 128), width)]),
        ],
        sems,
    )
    core = near("core", 1)
    greet([near("x", 1), near("x", -1), near("y", 1), near("y", -1), near("z", 1), near("z", -1), core])
    copies = Copies(send, recv)
    torus_start(copies, kv, 4, 3)
    ring_start(copies, "h", feat, width, tokens, 0)
    for key, (a, b) in zip(("wq", "wk", "wv"), places):
        copies.start(key, a, b, core)
    copies.start("wo", wo, wo2, core)
    torus_step(copies, kv, 4, 3, 1)
    ring_relay(copies, "h", feat, width, tokens, 0)
    torus_step(copies, kv, 4, 3, 2)
    torus_cross(copies, kv, 7, 0, 1, 7)
    torus_step(copies, kv, 4, 3, 3)

    copies.arrived(("h", "rr"))
    copies.arrived(("h", "ll"))
    for copy in own_weights:
        copy.wait()
    for key in ("wq", "wk", "wv"):
        copies.arrived(key)
    squares = jnp.zeros((tokens, 1), jnp.float32)
    for part in range(X):
        piece = feat[:, pl.ds(part * width, width)].astype(jnp.float32)
        squares = squares + jnp.sum(piece * piece, axis=1, keepdims=True)
    factor = lax.rsqrt(squares / (X * width) + NORM_EPS)
    for part in range(X):
        where = pl.ds(part * width, width)
        piece = feat[:, where].astype(jnp.float32)
        normed[:, where] = (piece * factor * gain[:, where].astype(jnp.float32)).astype(normed.dtype)
    product = jnp.dot(normed[...], wide[...], preferred_element_type=jnp.float32)

    def turned(head):
        part = product[:, head * dim : (head + 1) * dim]
        return (part * cosine[...] + pltpu.roll(part, dim // 2, 1) * sine[...]).astype(jnp.bfloat16)

    sk[0, 0, 0] = turned(heads)
    sk[0, 0, 1] = product[:, across + dim :].astype(jnp.bfloat16)
    for head in range(heads):
        queries[pl.ds(head * tokens, tokens), :] = turned(head)

    torus_step(copies, kv, 4, 3, 4)
    torus_cross(copies, kv, 7, 2, 6)
    later = Copies(send2, recv2)
    torus_start(later, sk, BACK, 0)

    def step(state, keys, values, bias):
        top, total, summed = state
        scores = lax.dot_general(
            queries[...], keys, (((1,), (1,)), ((), ())), preferred_element_type=jnp.float32
        ) * scale
        if bias is not None:
            scores = scores + bias
        new_top = jnp.maximum(top, jnp.max(scores, axis=1, keepdims=True))
        weights = jnp.exp(scores - new_top)
        shrink = jnp.exp(top - new_top)
        total = total * shrink + jnp.sum(weights, axis=1, keepdims=True)
        summed = summed * shrink + jnp.dot(
            weights.astype(jnp.bfloat16), values, preferred_element_type=jnp.float32
        )
        return new_top, total, summed

    def prefix(index, state):
        return step(state, kv[index, :, 0].reshape(-1, dim), kv[index, :, 1].reshape(-1, dim), None)

    def suffix(index, state):
        at = first[index, :][None, :]
        visible = (at >= own_start[...]) & (at <= token_index[...])
        bias = jnp.concatenate([jnp.where(visible, 0.0, MASKED)] * heads, axis=0)
        return step(state, sk[index, :, 0].reshape(-1, dim), sk[index, :, 1].reshape(-1, dim), bias)

    state = (
        jnp.full((rows, 1), MASKED, jnp.float32),
        jnp.zeros((rows, 1), jnp.float32),
        jnp.zeros((rows, dim), jnp.float32),
    )
    state = prefix(0, state)
    torus_cross(copies, kv, 7, 3, 5, 4)
    torus_step(later, sk, BACK, 0, 1)
    column(copies, "u")
    state = prefix(1, state)
    torus_step(later, sk, BACK, 0, 2)
    torus_cross(later, sk, BACK, 0)
    column(copies, "d")
    state = prefix(3, state)
    torus_cross(later, sk, BACK, 1, 2)
    column(copies, "v")
    state = prefix(2, state)
    state = suffix(0, state)
    column(later, "u")
    state = suffix(1, state)
    column(later, "d")
    state = suffix(3, state)
    column(later, "v")
    _, total, summed = suffix(2, state)
    result = summed / total
    for head in range(heads):
        out[:, head * dim : (head + 1) * dim] = result[head * tokens : (head + 1) * tokens].astype(out.dtype)
    copies.finish()
    later.finish()


def partner(slot, sign):
    tok = lax.axis_index("tok")
    grp = lax.axis_index("grp")
    dz, dy, dg = slot // 8, lax.rem(slot // 2, 4), lax.rem(slot, 2)
    z = lax.rem(tok // Y + Z + sign * dz, Z)
    y = lax.rem(lax.rem(tok, Y) + Y + sign * dy, Y)
    return {"grp": lax.rem(grp + dg, 2), "tok": z * Y + y}


def signal_all(more):
    barrier = pltpu.get_barrier_semaphore()

    def body(slot, carry):
        pl.semaphore_signal(barrier, inc=1, device_id=partner(slot, 1), device_id_type=MESH)
        return carry

    lax.fori_loop(1, 64, body, 0)
    for device in more:
        pl.semaphore_signal(barrier, inc=1, device_id=device, device_id_type=MESH)
    return barrier, 63 + len(more)


def experts_kernel(
    attended, hid, placed, gain, w_out, other_out, w_gate, w_up, w_down, back, mid,
    send, recv, sems, sent, came, sent_back, came_back, sent_part, came_part,
    outgoing, rows, hidden, results, wide, down, normed, wide_out, parts, got, transit,
):
    grp = lax.axis_index("grp")
    me = lax.axis_index("head")
    width = hid.shape[1]
    cap = placed.shape[0] // 64
    inner = w_gate.shape[1]
    many = 8 * cap
    columns = pl.ds(pl.multiple_of(me * width, 128), width)
    own_hidden = pl.ds(pl.multiple_of(me * inner, 128), inner)

    def block(slot):
        return pl.ds(pl.multiple_of(slot * cap, cap), cap)

    def there(slot):
        return pltpu.make_async_remote_copy(
            src_ref=outgoing.at[block(slot), :], dst_ref=rows.at[block(slot), columns],
            send_sem=sent.at[slot], recv_sem=came.at[slot],
            device_id=partner(slot, 1), device_id_type=MESH,
        )

    def home(slot):
        return pltpu.make_async_remote_copy(
            src_ref=results.at[block(slot), :], dst_ref=back.at[block(slot), :],
            send_sem=sent_back.at[slot], recv_sem=came_back.at[slot],
            device_id=partner(slot, -1), device_id_type=MESH,
        )

    def each(first, last, act):
        def body(slot, carry):
            act(slot)
            return carry

        lax.fori_loop(first, last, body, 0)

    def of_chunk(chunk, act):
        each(max(8 * chunk, 1), 8 * chunk + 8, act)

    weights = [
        pltpu.make_async_copy(w_gate, wide.at[:, pl.ds(0, inner)], sems.at[0]),
        pltpu.make_async_copy(w_up, wide.at[:, pl.ds(inner, inner)], sems.at[1]),
        pltpu.make_async_copy(w_down, down, sems.at[2]),
    ]
    own = pltpu.make_async_copy(outgoing.at[block(0), :], rows.at[block(0), columns], sems.at[3])
    half_out = w_out.shape[0]
    projections = [
        pltpu.make_async_copy(w_out, wide_out.at[0], sems.at[4]),
        pltpu.make_async_copy(other_out, wide_out.at[1], sems.at[5]),
    ]
    barrier, greetings = signal_all([near("x", 1), near("x", -1)])
    for copy in projections + weights:
        copy.start()
    for copy in projections:
        copy.wait()
    for side in range(2):
        for part in range(half_out // width):
            parts[2 * lax.rem(grp + side, 2) + part] = lax.dot_general(
                attended[...], wide_out[side, pl.ds(part * width, width), :],
                (((1,), (1,)), ((), ())), preferred_element_type=jnp.float32,
            ).astype(parts.dtype)
    pl.semaphore_wait(barrier, greetings)

    shares = Copies(sent_part, came_part)
    middle = parts.shape[1] // 2
    right, left, opposite = (lax.rem(me + d, X) for d in (1, 3, 2))
    upper, lower = pl.ds(0, middle), pl.ds(middle, middle)
    shares.start("tr", parts.at[opposite, upper], transit.at[0], near("x", 1))
    shares.start("tl", parts.at[opposite, lower], transit.at[1], near("x", -1))
    shares.start("r", parts.at[right], got.at[0], near("x", 1))
    shares.start("l", parts.at[left], got.at[2], near("x", -1))
    shares.arrived("tr")
    shares.start("rr", transit.at[0], got.at[1, upper], near("x", 1))
    shares.arrived("tl")
    shares.start("ll", transit.at[1], got.at[1, lower], near("x", -1))
    for key in ("r", "l", "rr", "ll"):
        shares.arrived(key)
    total = parts[me].astype(jnp.float32)
    for index in range(X - 1):
        total = total + got[index].astype(jnp.float32)
    mid[...] = (hid[...].astype(jnp.float32) + total).astype(mid.dtype)
    outgoing[...] = jnp.dot(
        placed[...], mid[...], preferred_element_type=jnp.float32
    ).astype(outgoing.dtype)
    shares.finish()
    for chunk in CHUNK_ORDER:
        of_chunk(chunk, lambda slot: there(slot).start())
    own.start()
    own.wait()
    for copy in weights:
        copy.wait()
    copies = Copies(send, recv)
    last = pltpu.make_async_copy(results.at[block(0), :], back.at[block(0), :], sems.at[3])

    def arrive(chunk):
        of_chunk(chunk, lambda slot: there(slot).wait_recv())
        ring_start(copies, ("m", chunk), rows, width, many, many * chunk)

    def pass_rows(chunk):
        ring_relay(copies, ("m", chunk), rows, width, many, many * chunk)

    def gate_up(chunk):
        copies.arrived((("m", chunk), "rr"))
        copies.arrived((("m", chunk), "ll"))
        at = pl.ds(many * chunk, many)
        squares = jnp.zeros((many, 1), jnp.float32)
        for part in range(X):
            piece = rows[at, pl.ds(part * width, width)].astype(jnp.float32)
            squares = squares + jnp.sum(piece * piece, axis=1, keepdims=True)
        factor = lax.rsqrt(squares / (X * width) + NORM_EPS)
        for part in range(X):
            where = pl.ds(part * width, width)
            piece = rows[at, where].astype(jnp.float32)
            normed[:, where] = (piece * factor * gain[:, where].astype(jnp.float32)).astype(normed.dtype)
        both = jnp.dot(normed[...], wide[...], preferred_element_type=jnp.float32)
        gate = both[:, :inner]
        hidden[at, own_hidden] = (gate / (1.0 + jnp.exp(-gate)) * both[:, inner:]).astype(hidden.dtype)

    def send_hidden(chunk):
        of_chunk(chunk, lambda slot: there(slot).wait_send())
        ring_start(copies, ("h", chunk), hidden, inner, many, many * chunk)

    def pass_hidden(chunk):
        ring_relay(copies, ("h", chunk), hidden, inner, many, many * chunk)

    def finish(chunk):
        copies.arrived((("h", chunk), "rr"))
        copies.arrived((("h", chunk), "ll"))
        at = pl.ds(many * chunk, many)
        results[at, :] = jnp.dot(
            hidden[at, :], down[...], preferred_element_type=jnp.float32
        ).astype(results.dtype)

    def send_home(chunk):
        if chunk == 0:
            last.start()
        of_chunk(chunk, lambda slot: home(slot).start())

    stages = ((arrive, 0), (pass_rows, 1), (gate_up, 2), (pass_hidden, 3), (send_hidden, 2), (send_home, 5), (finish, 4))
    for step in range(len(CHUNK_ORDER) + 5):
        for stage, lag in stages:
            if 0 <= step - lag < len(CHUNK_ORDER):
                stage(CHUNK_ORDER[step - lag])
    copies.finish()
    last.wait()
    each(1, 64, lambda slot: home(slot).wait())


def rotary_tables(token_positions, head_dim):
    half_dim = head_dim // 2
    frequency = jnp.exp(
        jnp.arange(half_dim, dtype=jnp.float32) * (-2.0 * math.log(ROPE_BASE) / head_dim)
    )
    angles = token_positions.astype(jnp.float32)[:, None] * frequency[None, :]
    return jnp.cos(angles), jnp.sin(angles)


def on_device(
    hidden_in,
    attn_gain,
    w_query,
    key_projection_weight,
    value_projection_weight,
    w_out,
    prefix_keys,
    cached_prefix_values,
    request_lengths,
    moe_gain,
    expert_ids,
    route_weights,
    w_gate,
    w_up,
    w_down,
):
    f32, bf16 = jnp.float32, jnp.bfloat16
    tok_count = lax.axis_size("tok")
    tok_rank = lax.axis_index("tok")
    grp_rank = lax.axis_index("grp")
    tok_dev = hidden_in.shape[1]
    model_width = attn_gain.shape[0]
    head_dim = prefix_keys.shape[3]
    prefix_dev = prefix_keys.shape[1]
    group_length = w_query.shape[1] // head_dim
    share = model_width // X
    quarter = hidden_in[0]

    lengths = request_lengths[0]
    request_ends = jnp.cumsum(lengths)
    starts = request_ends - lengths
    token_index = tok_rank * tok_dev + jnp.arange(tok_dev, dtype=jnp.int32)
    own_start = jnp.max(
        jnp.where(starts[None, :] <= token_index[:, None], starts[None, :], 0), axis=1
    )
    token_positions = prefix_dev * tok_count + token_index - own_start
    cosine, sine_part = rotary_tables(token_positions, head_dim)

    z_rank, y_rank = tok_rank // Y, tok_rank % Y
    y_from = (y_rank - jnp.arange(Y) + Y) % Y
    z_from = z_rank - jnp.arange(BACK + 1)
    device_from = jnp.where(z_from[None, :] >= 0, z_from[None, :] * Y + y_from[:, None], tok_count)
    key_index = (
        device_from[:, :, None] * tok_dev + jnp.arange(tok_dev, dtype=jnp.int32)
    ).reshape(Y, (BACK + 1) * tok_dev)
    attended, other_out = call(
        front_kernel, 0,
        (quarter, attn_gain[None, :], prefix_keys[0, :, 0], cached_prefix_values[0, :, 0], w_query,
         key_projection_weight, value_projection_weight, w_out,
         jnp.concatenate([cosine, cosine], axis=1), jnp.concatenate([-sine_part, sine_part], axis=1),
         own_start[:, None], token_index[:, None], key_index.astype(jnp.int32)),
        (shape(tok_dev, group_length * head_dim), shape(*w_out.shape)),
        [VM] * 4 + [HB] * 4 + [VM] * 5, [VM, HB], torus_copies(4, 3) + 8,
        (
            *[pltpu.SemaphoreType.DMA((torus_copies(BACK, 0),))] * 2,
            pltpu.VMEM((tok_dev, model_width), bf16),
            pltpu.VMEM((tok_dev, model_width), bf16),
            pltpu.VMEM((Y, Z, 2, prefix_dev, head_dim), bf16),
            pltpu.VMEM((Y, BACK + 1, 2, tok_dev, head_dim), bf16),
            pltpu.VMEM((model_width, (group_length + 2) * head_dim), bf16),
            pltpu.VMEM((group_length * tok_dev, head_dim), bf16),
        ),
    )

    experts = 2 * tok_count * w_gate.shape[0]
    top_count = expert_ids.shape[2]
    capacity = 4 * tok_dev * top_count // (3 * experts)
    chosen = expert_ids[0]
    e_grp, e_tok = chosen // tok_count, chosen % tok_count
    relative = (
        ((e_tok // Y - z_rank + Z) % Z) * 8
        + ((e_tok % Y - y_rank + Y) % Y) * 2
        + (e_grp + grp_rank) % 2
    )
    hit = relative[:, :, None] == jnp.arange(experts, dtype=jnp.int32)[None, None, :]
    uses = jnp.any(hit, axis=1)
    weight = jnp.sum(jnp.where(hit, route_weights[0][:, :, None], 0.0), axis=1)
    weight_hi = weight.astype(bf16)
    weight_lo = (weight - weight_hi.astype(f32)).astype(bf16)
    earlier = jnp.tril(jnp.ones((tok_dev, tok_dev), bf16), -1)
    rank = jnp.dot(earlier, uses.astype(bf16), preferred_element_type=f32)
    rank = jnp.where(uses, rank, -1.0).astype(bf16)
    slots = experts * capacity
    slot_index = jnp.arange(slots, dtype=jnp.int32)
    spread = (slot_index[None, :] // capacity == jnp.arange(experts, dtype=jnp.int32)[:, None]).astype(bf16)
    spread_rank = jnp.dot(rank, spread, preferred_element_type=f32)
    placed = spread_rank == (slot_index % capacity).astype(f32)[None, :]
    spread_rows = lax.dot_general(
        spread, rank, (((0,), (1,)), ((), ())), preferred_element_type=f32
    )
    placed_rows = (spread_rows == (slot_index % capacity).astype(f32)[:, None]).astype(bf16)

    inner = w_gate.shape[2]
    returned, mid = call(
        experts_kernel, 4,
        (attended, quarter, placed_rows, moe_gain[None, :], w_out, other_out, w_gate[0], w_up[0], w_down[0]),
        (shape(slots, share), shape(tok_dev, share)),
        [VM] * 4 + [HB] * 5, [VM] * 2, 2 * 8 * 4,
        (
            *[pltpu.SemaphoreType.DMA((64,))] * 4,
            *[pltpu.SemaphoreType.DMA((6,))] * 2,
            pltpu.VMEM((slots, share), bf16),
            pltpu.VMEM((slots, model_width), bf16),
            pltpu.VMEM((slots, X * inner), bf16),
            pltpu.VMEM((slots, share), bf16),
            pltpu.VMEM((model_width, 2 * inner), bf16),
            pltpu.VMEM((X * inner, share), bf16),
            pltpu.VMEM((8 * capacity, model_width), bf16),
            pltpu.VMEM((2, *w_out.shape), bf16),
            pltpu.VMEM((X, tok_dev, share), bf16),
            pltpu.VMEM((X - 1, tok_dev, share), bf16),
            pltpu.VMEM((2, tok_dev // 2, share), bf16),
        ),
    )

    def combine(part):
        spread_weight = jnp.where(placed, jnp.dot(part, spread, preferred_element_type=f32), 0.0)
        return jnp.dot(spread_weight.astype(bf16), returned, preferred_element_type=f32)

    output = (mid.astype(f32) + (combine(weight_hi) + combine(weight_lo))).astype(bf16)
    return output[None]


def solution(mesh):
    return jax.shard_map(
        on_device,
        mesh=mesh,
        in_specs=(
            P("grp", "tok", "head"),
            P(),
            P("grp", "head"),
            P("grp", "head"),
            P("grp", "head"),
            P("grp", "head"),
            P("grp", "tok", "head", None),
            P("grp", "tok", "head", None),
            P("grp", None),
            P(),
            P("grp", "tok", None),
            P("grp", "tok", None),
            P(("grp", "tok"), None, "head"),
            P(("grp", "tok"), None, "head"),
            P(("grp", "tok"), None, "head"),
        ),
        out_specs=P("grp", "tok", "head"),
        check_vma=False,
    )
```

```python
import functools
import math

import jax
import jax.numpy as jnp
from jax import lax
from jax.experimental import pallas as pl
from jax.experimental.pallas import tpu as pltpu
from jax.sharding import PartitionSpec as P

ROPE_BASE = 500000.0
NORM_EPS = 1e-06
MASKED = -1e30
MESH = pl.DeviceIdType.MESH
Z, Y, X = 8, 4, 4
CHUNK_ORDER = (0, 1, 5, 3, 4, 6, 2, 7)
BACK = 2


class Copies:
    def __init__(self, send, recv):
        self.send, self.recv, self.made, self.open = send, recv, {}, []

    def start(self, key, src, dst, device):
        at = len(self.made)
        copy = pltpu.make_async_remote_copy(
            src_ref=src, dst_ref=dst, send_sem=self.send.at[at], recv_sem=self.recv.at[at],
            device_id=device, device_id_type=MESH,
        )
        copy.start()
        self.made[key] = copy
        self.open.append(key)

    def arrived(self, key):
        self.made[key].wait_recv()
        self.open.remove(key)

    def finish(self):
        for key in list(self.open):
            self.arrived(key)
        for copy in self.made.values():
            copy.wait_send()


def near(axis, step):
    if axis == "x":
        return {"head": lax.rem(lax.axis_index("head") + (step + X), X)}
    if axis == "core":
        return {"grp": 1 - lax.axis_index("grp")}
    tok = lax.axis_index("tok")
    z, y = tok // Y, lax.rem(tok, Y)
    if axis == "z":
        z = lax.rem(z + (step + Z), Z)
    else:
        y = lax.rem(y + (step + Y), Y)
    return {"tok": z * Y + y}


def greet(devices):
    barrier = pltpu.get_barrier_semaphore()
    for device in devices:
        pl.semaphore_signal(barrier, inc=1, device_id=device, device_id_type=MESH)
    pl.semaphore_wait(barrier, len(devices))


def torus_start(copies, kv, forward, backward):
    up, down = near("y", 1), near("y", -1)
    if forward:
        copies.start(("f", 1), kv.at[0, 0], kv.at[0, 1], near("z", 1))
    if backward:
        copies.start(("b", 1), kv.at[0, 0], kv.at[0, forward + backward], near("z", -1))
    copies.start(("u", 0), kv.at[0, 0], kv.at[1, 0], up)
    copies.start(("d", 0), kv.at[0, 0], kv.at[3, 0], down)


def torus_step(copies, kv, forward, backward, step):
    up, down = near("y", 1), near("y", -1)
    last = forward + backward
    for mark, reach, slot, following, way in (
        ("f", forward, step, step + 1, 1),
        ("b", backward, last + 1 - step, last - step, -1),
    ):
        if step > reach:
            continue
        copies.arrived((mark, step))
        if step < reach:
            copies.start((mark, step + 1), kv.at[0, slot], kv.at[0, following], near("z", way))
        copies.start(("u", slot), kv.at[0, slot], kv.at[1, slot], up)
        copies.start(("d", slot), kv.at[0, slot], kv.at[3, slot], down)


def torus_cross(copies, kv, last, *slots):
    for slot in slots:
        if slot <= (last + 1) // 2:
            copies.arrived(("u", slot))
            copies.start(("v", slot), kv.at[1, slot], kv.at[2, slot], near("y", 1))
        else:
            copies.arrived(("d", slot))
            copies.start(("v", slot), kv.at[3, slot], kv.at[2, slot], near("y", -1))


def column(copies, mark):
    for key in [key for key in copies.open if key[0] == mark]:
        copies.arrived(key)


def torus_copies(forward, backward):
    slots = forward + backward + 1
    return forward + backward + 3 * slots


def ring_start(copies, key, ref, width, rows, offset):
    me = lax.axis_index("head")
    own = ref.at[pl.ds(offset, rows), pl.ds(pl.multiple_of(me * width, 128), width)]
    copies.start((key, "r"), own, own, near("x", 1))
    copies.start((key, "l"), own, own, near("x", -1))


def ring_relay(copies, key, ref, width, rows, offset):
    me = lax.axis_index("head")
    half = rows // 2
    copies.arrived((key, "r"))
    left = lax.rem(me + (X - 1), X)
    first = ref.at[pl.ds(offset, half), pl.ds(pl.multiple_of(left * width, 128), width)]
    copies.start((key, "rr"), first, first, near("x", 1))
    copies.arrived((key, "l"))
    right = lax.rem(me + 1, X)
    second = ref.at[pl.ds(offset + half, half), pl.ds(pl.multiple_of(right * width, 128), width)]
    copies.start((key, "ll"), second, second, near("x", -1))


def local(pairs, sems):
    made = [pltpu.make_async_copy(a, b, sems.at[i]) for i, (a, b) in enumerate(pairs)]
    for copy in made:
        copy.start()
    for copy in made:
        copy.wait()


VM = pl.BlockSpec(memory_space=pltpu.VMEM)
HB = pl.BlockSpec(memory_space=pl.ANY)


def call(kernel, ident, ins, outs, in_specs, out_specs, copies, extra=()):
    return pl.pallas_call(
        kernel,
        out_shape=outs,
        in_specs=in_specs,
        out_specs=out_specs,
        scratch_shapes=[
            pltpu.SemaphoreType.DMA((copies,)),
            pltpu.SemaphoreType.DMA((copies,)),
            pltpu.SemaphoreType.DMA((6,)),
            *extra,
        ],
        compiler_params=pltpu.CompilerParams(collective_id=ident, has_side_effects=True),
    )(*ins)


def shape(*dims, dtype=jnp.bfloat16):
    return jax.ShapeDtypeStruct(dims, dtype)


def front_kernel(
    hid, gain, pk, pv, wq, wk, wv, wo, cosine, sine, own_start, token_index, first, out, wo2,
    send, recv, sems, send2, recv2, feat, normed, kv, sk, wide, queries,
):
    me, grp = lax.axis_index("head"), lax.axis_index("grp")
    tokens, width = hid.shape
    depth, across = wq.shape
    dim = pk.shape[1]
    heads = across // dim
    rows = heads * tokens
    scale = dim ** (-0.5)
    mine = pl.ds(pl.multiple_of(grp * depth, depth), depth)
    places = [
        (wq, wide.at[mine, pl.ds(0, across)]),
        (wk, wide.at[mine, pl.ds(across, dim)]),
        (wv, wide.at[mine, pl.ds(across + dim, dim)]),
    ]
    own_weights = [pltpu.make_async_copy(a, b, sems.at[3 + i]) for i, (a, b) in enumerate(places)]
    for copy in own_weights:
        copy.start()
    local(
        [
            (pk, kv.at[0, 0, 0]),
            (pv, kv.at[0, 0, 1]),
            (hid, feat.at[:, pl.ds(pl.multiple_of(me * width, 128), width)]),
        ],
        sems,
    )
    core = near("core", 1)
    greet([near("x", 1), near("x", -1), near("y", 1), near("y", -1), near("z", 1), near("z", -1), core])
    copies = Copies(send, recv)
    torus_start(copies, kv, 4, 3)
    ring_start(copies, "h", feat, width, tokens, 0)
    for key, (a, b) in zip(("wq", "wk", "wv"), places):
        copies.start(key, a, b, core)
    copies.start("wo", wo, wo2, core)
    torus_step(copies, kv, 4, 3, 1)
    ring_relay(copies, "h", feat, width, tokens, 0)
    torus_step(copies, kv, 4, 3, 2)
    torus_cross(copies, kv, 7, 0, 1, 7)
    torus_step(copies, kv, 4, 3, 3)

    copies.arrived(("h", "rr"))
    copies.arrived(("h", "ll"))
    for copy in own_weights:
        copy.wait()
    for key in ("wq", "wk", "wv"):
        copies.arrived(key)
    squares = jnp.zeros((tokens, 1), jnp.float32)
    for part in range(X):
        piece = feat[:, pl.ds(part * width, width)].astype(jnp.float32)
        squares = squares + jnp.sum(piece * piece, axis=1, keepdims=True)
    factor = lax.rsqrt(squares / (X * width) + NORM_EPS)
    for part in range(X):
        where = pl.ds(part * width, width)
        piece = feat[:, where].astype(jnp.float32)
        normed[:, where] = (piece * factor * gain[:, where].astype(jnp.float32)).astype(normed.dtype)
    product = jnp.dot(normed[...], wide[...], preferred_element_type=jnp.float32)

    def turned(head):
        part = product[:, head * dim : (head + 1) * dim]
        return (part * cosine[...] + pltpu.roll(part, dim // 2, 1) * sine[...]).astype(jnp.bfloat16)

    sk[0, 0, 0] = turned(heads)
    sk[0, 0, 1] = product[:, across + dim :].astype(jnp.bfloat16)
    for head in range(heads):
        queries[pl.ds(head * tokens, tokens), :] = turned(head)

    torus_step(copies, kv, 4, 3, 4)
    torus_cross(copies, kv, 7, 2, 6)
    later = Copies(send2, recv2)
    torus_start(later, sk, BACK, 0)

    def step(state, keys, values, bias):
        top, total, summed = state
        scores = lax.dot_general(
            queries[...], keys, (((1,), (1,)), ((), ())), preferred_element_type=jnp.float32
        ) * scale
        if bias is not None:
            scores = scores + bias
        new_top = jnp.maximum(top, jnp.max(scores, axis=1, keepdims=True))
        weights = jnp.exp(scores - new_top)
        shrink = jnp.exp(top - new_top)
        total = total * shrink + jnp.sum(weights, axis=1, keepdims=True)
        summed = summed * shrink + jnp.dot(
            weights.astype(jnp.bfloat16), values, preferred_element_type=jnp.float32
        )
        return new_top, total, summed

    def prefix(index, state):
        return step(state, kv[index, :, 0].reshape(-1, dim), kv[index, :, 1].reshape(-1, dim), None)

    def suffix(index, state):
        at = first[index, :][None, :]
        visible = (at >= own_start[...]) & (at <= token_index[...])
        bias = jnp.concatenate([jnp.where(visible, 0.0, MASKED)] * heads, axis=0)
        return step(state, sk[index, :, 0].reshape(-1, dim), sk[index, :, 1].reshape(-1, dim), bias)

    state = (
        jnp.full((rows, 1), MASKED, jnp.float32),
        jnp.zeros((rows, 1), jnp.float32),
        jnp.zeros((rows, dim), jnp.float32),
    )
    state = prefix(0, state)
    torus_cross(copies, kv, 7, 3, 5, 4)
    torus_step(later, sk, BACK, 0, 1)
    column(copies, "u")
    state = prefix(1, state)
    torus_step(later, sk, BACK, 0, 2)
    torus_cross(later, sk, BACK, 0)
    column(copies, "d")
    state = prefix(3, state)
    torus_cross(later, sk, BACK, 1, 2)
    column(copies, "v")
    state = prefix(2, state)
    state = suffix(0, state)
    column(later, "u")
    state = suffix(1, state)
    column(later, "d")
    state = suffix(3, state)
    column(later, "v")
    _, total, summed = suffix(2, state)
    result = summed / total
    for head in range(heads):
        out[:, head * dim : (head + 1) * dim] = result[head * tokens : (head + 1) * tokens].astype(out.dtype)
    copies.finish()
    later.finish()


def partner(slot, sign):
    tok = lax.axis_index("tok")
    grp = lax.axis_index("grp")
    dz, dy, dg = slot // 8, lax.rem(slot // 2, 4), lax.rem(slot, 2)
    z = lax.rem(tok // Y + Z + sign * dz, Z)
    y = lax.rem(lax.rem(tok, Y) + Y + sign * dy, Y)
    return {"grp": lax.rem(grp + dg, 2), "tok": z * Y + y}


def signal_all(more):
    barrier = pltpu.get_barrier_semaphore()

    def body(slot, carry):
        pl.semaphore_signal(barrier, inc=1, device_id=partner(slot, 1), device_id_type=MESH)
        return carry

    lax.fori_loop(1, 64, body, 0)
    for device in more:
        pl.semaphore_signal(barrier, inc=1, device_id=device, device_id_type=MESH)
    return barrier, 63 + len(more)


def experts_kernel(
    attended, hid, placed, gain, w_out, other_out, w_gate, w_up, w_down, back, mid,
    send, recv, sems, sent, came, sent_back, came_back, sent_part, came_part,
    outgoing, rows, hidden, results, wide, down, normed, wide_out, parts, got, transit,
):
    grp = lax.axis_index("grp")
    me = lax.axis_index("head")
    width = hid.shape[1]
    cap = placed.shape[0] // 64
    inner = w_gate.shape[1]
    many = 8 * cap
    columns = pl.ds(pl.multiple_of(me * width, 128), width)
    own_hidden = pl.ds(pl.multiple_of(me * inner, 128), inner)

    def block(slot):
        return pl.ds(pl.multiple_of(slot * cap, cap), cap)

    def there(slot):
        return pltpu.make_async_remote_copy(
            src_ref=outgoing.at[block(slot), :], dst_ref=rows.at[block(slot), columns],
            send_sem=sent.at[slot], recv_sem=came.at[slot],
            device_id=partner(slot, 1), device_id_type=MESH,
        )

    def home(slot):
        return pltpu.make_async_remote_copy(
            src_ref=results.at[block(slot), :], dst_ref=back.at[block(slot), :],
            send_sem=sent_back.at[slot], recv_sem=came_back.at[slot],
            device_id=partner(slot, -1), device_id_type=MESH,
        )

    def each(first, last, act):
        def body(slot, carry):
            act(slot)
            return carry

        lax.fori_loop(first, last, body, 0)

    def of_chunk(chunk, act):
        each(max(8 * chunk, 1), 8 * chunk + 8, act)

    weights = [
        pltpu.make_async_copy(w_gate, wide.at[:, pl.ds(0, inner)], sems.at[0]),
        pltpu.make_async_copy(w_up, wide.at[:, pl.ds(inner, inner)], sems.at[1]),
        pltpu.make_async_copy(w_down, down, sems.at[2]),
    ]
    own = pltpu.make_async_copy(outgoing.at[block(0), :], rows.at[block(0), columns], sems.at[3])
    half_out = w_out.shape[0]
    projections = [
        pltpu.make_async_copy(w_out, wide_out.at[0], sems.at[4]),
        pltpu.make_async_copy(other_out, wide_out.at[1], sems.at[5]),
    ]
    barrier, greetings = signal_all([near("x", 1), near("x", -1)])
    for copy in projections + weights:
        copy.start()
    for copy in projections:
        copy.wait()
    for side in range(2):
        for part in range(half_out // width):
            parts[2 * lax.rem(grp + side, 2) + part] = lax.dot_general(
                attended[...], wide_out[side, pl.ds(part * width, width), :],
                (((1,), (1,)), ((), ())), preferred_element_type=jnp.float32,
            ).astype(parts.dtype)
    pl.semaphore_wait(barrier, greetings)

    shares = Copies(sent_part, came_part)
    middle = parts.shape[1] // 2
    right, left, opposite = (lax.rem(me + d, X) for d in (1, 3, 2))
    upper, lower = pl.ds(0, middle), pl.ds(middle, middle)
    shares.start("tr", parts.at[opposite, upper], transit.at[0], near("x", 1))
    shares.start("tl", parts.at[opposite, lower], transit.at[1], near("x", -1))
    shares.start("r", parts.at[right], got.at[0], near("x", 1))
    shares.start("l", parts.at[left], got.at[2], near("x", -1))
    shares.arrived("tr")
    shares.start("rr", transit.at[0], got.at[1, upper], near("x", 1))
    shares.arrived("tl")
    shares.start("ll", transit.at[1], got.at[1, lower], near("x", -1))
    for key in ("r", "l", "rr", "ll"):
        shares.arrived(key)
    total = parts[me].astype(jnp.float32)
    for index in range(X - 1):
        total = total + got[index].astype(jnp.float32)
    mid[...] = (hid[...].astype(jnp.float32) + total).astype(mid.dtype)
    outgoing[...] = jnp.dot(
        placed[...], mid[...], preferred_element_type=jnp.float32
    ).astype(outgoing.dtype)
    shares.finish()
    there(8 * CHUNK_ORDER[1]).start()
    for one, two in zip(CHUNK_ORDER[0::2], CHUNK_ORDER[1::2]):
        def both_ways(index, carry):
            there(8 * one + index).start()
            there(8 * two + index).start()
            return carry

        lax.fori_loop(0 if one else 1, 8, both_ways, 0)
    own.start()
    own.wait()
    for copy in weights:
        copy.wait()
    copies = Copies(send, recv)
    last = pltpu.make_async_copy(results.at[block(0), :], back.at[block(0), :], sems.at[3])

    def arrive(chunk):
        of_chunk(chunk, lambda slot: there(slot).wait_recv())
        ring_start(copies, ("m", chunk), rows, width, many, many * chunk)

    def pass_rows(chunk):
        ring_relay(copies, ("m", chunk), rows, width, many, many * chunk)

    def gate_up(chunk):
        copies.arrived((("m", chunk), "rr"))
        copies.arrived((("m", chunk), "ll"))
        at = pl.ds(many * chunk, many)
        squares = jnp.zeros((many, 1), jnp.float32)
        for part in range(X):
            piece = rows[at, pl.ds(part * width, width)].astype(jnp.float32)
            squares = squares + jnp.sum(piece * piece, axis=1, keepdims=True)
        factor = lax.rsqrt(squares / (X * width) + NORM_EPS)
        for part in range(X):
            where = pl.ds(part * width, width)
            piece = rows[at, where].astype(jnp.float32)
            normed[:, where] = (piece * factor * gain[:, where].astype(jnp.float32)).astype(normed.dtype)
        both = jnp.dot(normed[...], wide[...], preferred_element_type=jnp.float32)
        gate = both[:, :inner]
        hidden[at, own_hidden] = (gate / (1.0 + jnp.exp(-gate)) * both[:, inner:]).astype(hidden.dtype)

    def send_hidden(chunk):
        of_chunk(chunk, lambda slot: there(slot).wait_send())
        ring_start(copies, ("h", chunk), hidden, inner, many, many * chunk)

    def pass_hidden(chunk):
        ring_relay(copies, ("h", chunk), hidden, inner, many, many * chunk)

    def finish(chunk):
        copies.arrived((("h", chunk), "rr"))
        copies.arrived((("h", chunk), "ll"))
        at = pl.ds(many * chunk, many)
        results[at, :] = jnp.dot(
            hidden[at, :], down[...], preferred_element_type=jnp.float32
        ).astype(results.dtype)

    def send_home(chunk):
        if chunk == 0:
            last.start()
        of_chunk(chunk, lambda slot: home(slot).start())

    stages = ((arrive, 0), (pass_rows, 1), (gate_up, 2), (pass_hidden, 3), (send_hidden, 2), (send_home, 5), (finish, 4))
    for step in range(len(CHUNK_ORDER) + 5):
        for stage, lag in stages:
            if 0 <= step - lag < len(CHUNK_ORDER):
                stage(CHUNK_ORDER[step - lag])
    copies.finish()
    last.wait()
    each(1, 64, lambda slot: home(slot).wait())


def rotary_tables(token_positions, head_dim):
    half_dim = head_dim // 2
    frequency = jnp.exp(
        jnp.arange(half_dim, dtype=jnp.float32) * (-2.0 * math.log(ROPE_BASE) / head_dim)
    )
    angles = token_positions.astype(jnp.float32)[:, None] * frequency[None, :]
    return jnp.cos(angles), jnp.sin(angles)


def on_device(
    hidden_in,
    attn_gain,
    w_query,
    key_projection_weight,
    value_projection_weight,
    w_out,
    prefix_keys,
    cached_prefix_values,
    request_lengths,
    moe_gain,
    expert_ids,
    route_weights,
    w_gate,
    w_up,
    w_down,
):
    f32, bf16 = jnp.float32, jnp.bfloat16
    tok_count = lax.axis_size("tok")
    tok_rank = lax.axis_index("tok")
    grp_rank = lax.axis_index("grp")
    tok_dev = hidden_in.shape[1]
    model_width = attn_gain.shape[0]
    head_dim = prefix_keys.shape[3]
    prefix_dev = prefix_keys.shape[1]
    group_length = w_query.shape[1] // head_dim
    share = model_width // X
    quarter = hidden_in[0]

    lengths = request_lengths[0]
    request_ends = jnp.cumsum(lengths)
    starts = request_ends - lengths
    token_index = tok_rank * tok_dev + jnp.arange(tok_dev, dtype=jnp.int32)
    own_start = jnp.max(
        jnp.where(starts[None, :] <= token_index[:, None], starts[None, :], 0), axis=1
    )
    token_positions = prefix_dev * tok_count + token_index - own_start
    cosine, sine_part = rotary_tables(token_positions, head_dim)

    z_rank, y_rank = tok_rank // Y, tok_rank % Y
    y_from = (y_rank - jnp.arange(Y) + Y) % Y
    z_from = z_rank - jnp.arange(BACK + 1)
    device_from = jnp.where(z_from[None, :] >= 0, z_from[None, :] * Y + y_from[:, None], tok_count)
    key_index = (
        device_from[:, :, None] * tok_dev + jnp.arange(tok_dev, dtype=jnp.int32)
    ).reshape(Y, (BACK + 1) * tok_dev)
    attended, other_out = call(
        front_kernel, 0,
        (quarter, attn_gain[None, :], prefix_keys[0, :, 0], cached_prefix_values[0, :, 0], w_query,
         key_projection_weight, value_projection_weight, w_out,
         jnp.concatenate([cosine, cosine], axis=1), jnp.concatenate([-sine_part, sine_part], axis=1),
         own_start[:, None], token_index[:, None], key_index.astype(jnp.int32)),
        (shape(tok_dev, group_length * head_dim), shape(*w_out.shape)),
        [VM] * 4 + [HB] * 4 + [VM] * 5, [VM, HB], torus_copies(4, 3) + 8,
        (
            *[pltpu.SemaphoreType.DMA((torus_copies(BACK, 0),))] * 2,
            pltpu.VMEM((tok_dev, model_width), bf16),
            pltpu.VMEM((tok_dev, model_width), bf16),
            pltpu.VMEM((Y, Z, 2, prefix_dev, head_dim), bf16),
            pltpu.VMEM((Y, BACK + 1, 2, tok_dev, head_dim), bf16),
            pltpu.VMEM((model_width, (group_length + 2) * head_dim), bf16),
            pltpu.VMEM((group_length * tok_dev, head_dim), bf16),
        ),
    )

    experts = 2 * tok_count * w_gate.shape[0]
    top_count = expert_ids.shape[2]
    capacity = 4 * tok_dev * top_count // (3 * experts)
    chosen = expert_ids[0]
    e_grp, e_tok = chosen // tok_count, chosen % tok_count
    relative = (
        ((e_tok // Y - z_rank + Z) % Z) * 8
        + ((e_tok % Y - y_rank + Y) % Y) * 2
        + (e_grp + grp_rank) % 2
    )
    hit = relative[:, :, None] == jnp.arange(experts, dtype=jnp.int32)[None, None, :]
    uses = jnp.any(hit, axis=1)
    weight = jnp.sum(jnp.where(hit, route_weights[0][:, :, None], 0.0), axis=1)
    weight_hi = weight.astype(bf16)
    weight_lo = (weight - weight_hi.astype(f32)).astype(bf16)
    earlier = jnp.tril(jnp.ones((tok_dev, tok_dev), bf16), -1)
    rank = jnp.dot(earlier, uses.astype(bf16), preferred_element_type=f32)
    rank = jnp.where(uses, rank, -1.0).astype(bf16)
    slots = experts * capacity
    slot_index = jnp.arange(slots, dtype=jnp.int32)
    spread = (slot_index[None, :] // capacity == jnp.arange(experts, dtype=jnp.int32)[:, None]).astype(bf16)
    spread_rank = jnp.dot(rank, spread, preferred_element_type=f32)
    placed = spread_rank == (slot_index % capacity).astype(f32)[None, :]
    spread_rows = lax.dot_general(
        spread, rank, (((0,), (1,)), ((), ())), preferred_element_type=f32
    )
    placed_rows = (spread_rows == (slot_index % capacity).astype(f32)[:, None]).astype(bf16)

    inner = w_gate.shape[2]
    returned, mid = call(
        experts_kernel, 4,
        (attended, quarter, placed_rows, moe_gain[None, :], w_out, other_out, w_gate[0], w_up[0], w_down[0]),
        (shape(slots, share), shape(tok_dev, share)),
        [VM] * 4 + [HB] * 5, [VM] * 2, 2 * 8 * 4,
        (
            *[pltpu.SemaphoreType.DMA((64,))] * 4,
            *[pltpu.SemaphoreType.DMA((6,))] * 2,
            pltpu.VMEM((slots, share), bf16),
            pltpu.VMEM((slots, model_width), bf16),
            pltpu.VMEM((slots, X * inner), bf16),
            pltpu.VMEM((slots, share), bf16),
            pltpu.VMEM((model_width, 2 * inner), bf16),
            pltpu.VMEM((X * inner, share), bf16),
            pltpu.VMEM((8 * capacity, model_width), bf16),
            pltpu.VMEM((2, *w_out.shape), bf16),
            pltpu.VMEM((X, tok_dev, share), bf16),
            pltpu.VMEM((X - 1, tok_dev, share), bf16),
            pltpu.VMEM((2, tok_dev // 2, share), bf16),
        ),
    )

    def combine(part):
        spread_weight = jnp.where(placed, jnp.dot(part, spread, preferred_element_type=f32), 0.0)
        return jnp.dot(spread_weight.astype(bf16), returned, preferred_element_type=f32)

    output = (mid.astype(f32) + (combine(weight_hi) + combine(weight_lo))).astype(bf16)
    return output[None]


def solution(mesh):
    return jax.shard_map(
        on_device,
        mesh=mesh,
        in_specs=(
            P("grp", "tok", "head"),
            P(),
            P("grp", "head"),
            P("grp", "head"),
            P("grp", "head"),
            P("grp", "head"),
            P("grp", "tok", "head", None),
            P("grp", "tok", "head", None),
            P("grp", None),
            P(),
            P("grp", "tok", None),
            P("grp", "tok", None),
            P(("grp", "tok"), None, "head"),
            P(("grp", "tok"), None, "head"),
            P(("grp", "tok"), None, "head"),
        ),
        out_specs=P("grp", "tok", "head"),
        check_vma=False,
    )
```
